32 devices in a mesh: sfc: 16 (over z, y, x), lev: 2 (over core).
Axes of the slice: x: 2, y: 2, z: 4, core: 2. Of those that a mesh axis runs over, the one named last changes fastest.
Arguments:
- air_state: float32 [24, 8, 32768], P(None, 'lev', 'sfc'), may hold values from -6 to 6
- metric: float32 [2, 2048], P(None, 'sfc'), may hold values from -5 to 5
- jacobian: float32 [2048], P('sfc'), may hold values from 0.25 to 4
- edge_nbr: int32 [4, 2048], P(None, 'sfc'), may hold values from 0 to 2047, as said below
- edge_side: int32 [4, 2048], P(None, 'sfc'), may hold values from 0 to 3
- coszen: float32 [32768], P('sfc'), may hold values from -1 to 1
- kappa_base: float32 [112], replicated, may hold values from 0.02 to 2
- band_kappa: float32 [112, 20], replicated, may hold values from 0.005 to 0.2
- solar_weight: float32 [112], replicated, may hold values from 0.5 to 2
- stretch_pos: int32 [32768], P('sfc'), may hold values from 0 to 32767, as said below
- stretch_src: int32 [32768], P('sfc'), may hold values from 0 to 32767, as said below
Outputs:
- new_state: float32 [24, 8, 32768], P(None, 'lev', 'sfc')
- surface_flux: float32 [32768], P(('sfc', 'lev'))
The draws below stay inside these ranges and needn't reach their ends.
Inputs may be any that keep to these rules, and one draw needn't show every extreme that they name: edge_nbr[k, g] lies within 128 elements of g along the curve, cyclically over 2048 elements; that distance is reached. stretch_pos is a permutation of the columns and stretch_src its inverse; column c belongs to the stretch of device stretch_pos[c] // 2048; each device receives 2048 columns, at most 256 of them from one device, a bound reached in every draw; the columns that one device sends to one device take consecutive stretch positions. `stretch_src`: the inverse of stretch_pos.
All inputs are finite; a program needn't handle non-finite values.
Results may differ from the reference program's by a relative error of at most 0.0001.
Values sent between devices are 32-bit elements; how exact they have to be, the bound alone decides.
A program may use at most 64 MiB of HBM per device.

```python
import math
import jax
import jax.numpy as jnp
import numpy as np
from jax import lax

NODES = 16
E_DEV = 128
TRACERS = 20
GPOINTS = 112
GBLOCK = 16
FIELDS = 24
LEVELS = 8
ELEMS = 2048
COLS_DEV = 2048
COLUMNS = 32768
N_SFC = 16


def stretch_tables(key):
    sfc_devices = N_SFC
    local_cols = NODES * E_DEV
    even_share = local_cols // sfc_devices
    pair_count = sfc_devices // 2
    key_list = jax.random.split(jax.random.fold_in(key, 7), 3)
    shuffle_order = jax.random.permutation(key_list[0], sfc_devices).astype(jnp.int32)
    amounts = jax.random.randint(key_list[1], (pair_count,), 0, even_share + 1).astype(jnp.int32)
    amounts = amounts.at[0].set(even_share)
    shift_extra = jnp.zeros((sfc_devices,), jnp.int32).at[shuffle_order[0::2]].set(amounts)
    shift_extra = shift_extra.at[shuffle_order[1::2]].set(-amounts)
    source_ids = jnp.arange(sfc_devices, dtype=jnp.int32)[:, None]
    target_ids = jnp.arange(sfc_devices, dtype=jnp.int32)[None, :]
    sizes_table = even_share + shift_extra[jnp.mod(target_ids - source_ids, sfc_devices)]
    inclusive = jnp.cumsum(sizes_table, axis=1).astype(jnp.int32)
    starts = inclusive - sizes_table
    offsets = (jnp.cumsum(sizes_table, axis=0) - sizes_table).astype(jnp.int32)
    slot_range = jnp.arange(local_cols, dtype=jnp.int32)
    destination = jax.vmap(lambda cum_row: jnp.searchsorted(cum_row, slot_range, side='right'))(inclusive).astype(jnp.int32)
    start_of = jnp.take_along_axis(starts, destination, axis=1)
    offset_of = jnp.take_along_axis(offsets, destination, axis=1)
    position = destination * local_cols + offset_of + slot_range[None, :] - start_of
    shuffles = jax.vmap(lambda sub_key: jax.random.permutation(sub_key, local_cols))(jax.random.split(key_list[2], sfc_devices)).astype(jnp.int32)
    column = source_ids * local_cols + shuffles
    all_columns = sfc_devices * local_cols
    forward = jnp.zeros((all_columns,), jnp.int32).at[column.reshape(-1)].set(position.reshape(-1).astype(jnp.int32))
    backward = jnp.zeros((all_columns,), jnp.int32).at[position.reshape(-1)].set(column.reshape(-1))
    return (forward, backward)


def draw_stretch_pos(key, part):
    return stretch_tables(key)[0]


def draw_stretch_src(key, part):
    return stretch_tables(key)[1]


def draw_edge_nbr(key, part):
    element_total = N_SFC * E_DEV
    curve_steps = jax.random.randint(jax.random.fold_in(key, 3), (4, element_total), -E_DEV, E_DEV + 1).astype(jnp.int32)
    curve_steps = curve_steps.at[0, 0].set(E_DEV)
    return jnp.mod(jnp.arange(element_total, dtype=jnp.int32)[None, :] + curve_steps, element_total).astype(jnp.int32)


def set_ends(values, own_key, least, largest):
    longest = values.shape.index(max(values.shape))
    spots = []
    for shift in (0, 1):
        where = [jax.random.randint(jax.random.fold_in(own_key, axis), (), 0, length) for axis, length in enumerate(values.shape)]
        where[longest] = (where[longest] + shift) % values.shape[longest]
        spots.append(tuple(where))
    return values.at[spots[0]].set(least).at[spots[1]].set(largest)


def levels(rng, shape, cuts, low, largest):
    loudness = 1.0
    for axis_at, blocks in cuts:
        draws = jax.random.uniform(jax.random.fold_in(jax.random.fold_in(rng, 6), axis_at), (blocks,), jnp.float32, low / len(cuts), largest / len(cuts))
        loudness = loudness * jnp.repeat(jnp.exp(draws), shape[axis_at] // blocks).reshape((-1,) + (1,) * (len(shape) - 1 - axis_at))
    return loudness


def bell_draw(rng, dims, width, bound, cuts=(), kind=jnp.bfloat16):
    result = jax.random.normal(rng, dims, jnp.float32) * width
    if len(cuts) > 0:
        result = levels(rng, dims, cuts, -0.22, 0.18) * result
    return jnp.clip(result, min=-bound, max=bound).astype(kind)


def setup_inputs(seed: int = 0) -> dict:
    streams_of = jax.random.split(jax.random.key(seed), 12)
    air_state = bell_draw(streams_of[0], (FIELDS, LEVELS, COLUMNS), 1.0, 6.0, ((1, 2), (2, 16)), jnp.float32)
    metric = bell_draw(streams_of[1], (2, ELEMS), 1.0, 5.0, ((1, 16),), jnp.float32)
    jacobian = jnp.clip(jnp.exp(math.log(4.0) - 2.7725887 * jax.random.uniform(streams_of[2], (ELEMS,), jnp.float32) ** levels(streams_of[2], (ELEMS,), ((0, 16),), -0.2, 0.2)), 0.25, 4.0)
    edge_nbr = draw_edge_nbr(jax.random.fold_in(streams_of[11], 71), 0)
    edge_side = set_ends(jax.random.randint(streams_of[4], (4, ELEMS), 0, 4), jax.random.fold_in(streams_of[4], 1), 0, 3).astype(jnp.int32)
    coszen = jnp.clip(jax.random.uniform(streams_of[5], (COLUMNS,), jnp.float32, -1.0, 1.0) * levels(streams_of[5], (COLUMNS,), ((0, 16),), -0.4, 0.0), -1.0, 1.0)
    kappa_base = jnp.clip(jnp.exp(jax.random.uniform(streams_of[6], (GPOINTS,), jnp.float32, math.log(0.02), math.log(2.0))), 0.02, 2.0)
    band_kappa = jnp.clip(jnp.exp(jax.random.uniform(streams_of[7], (GPOINTS, TRACERS), jnp.float32, math.log(0.005), math.log(0.2))), 0.005, 0.2)
    solar_weight = jnp.clip(jnp.exp(jax.random.uniform(streams_of[8], (GPOINTS,), jnp.float32, math.log(0.5), math.log(2.0))), 0.5, 2.0)
    stretch_pos = draw_stretch_pos(jax.random.fold_in(streams_of[11], 71), 0)
    stretch_src = draw_stretch_src(jax.random.fold_in(streams_of[11], 71), 0)
    return dict(air_state=air_state, metric=metric, jacobian=jacobian, edge_nbr=edge_nbr, edge_side=edge_side, coszen=coszen, kappa_base=kappa_base, band_kappa=band_kappa, solar_weight=solar_weight, stretch_pos=stretch_pos, stretch_src=stretch_src)


GLL_POINTS = np.array([-1.0, -1.0 / np.sqrt(5.0), 1.0 / np.sqrt(5.0), 1.0])
EDGE_NODES = np.array([[4, 8], [13, 14], [11, 7], [2, 1]], dtype=np.int32)
STEP_DYN = 0.2
DEPTH_UNIT = 0.05
HEAT_SCALE = 0.1
FLUX_SCALE = 0.02

def derivative_tables():
    spacing = GLL_POINTS[:, None] - GLL_POINTS[None, :]
    unit_diag = np.eye(4)
    safe_space = np.where(unit_diag > 0, 1.0, spacing)
    weights_row = np.prod(safe_space, axis=1)
    derivative = weights_row[:, None] / weights_row[None, :] / safe_space
    inverse_gap = np.where(unit_diag > 0, 0.0, 1.0 / safe_space)
    derivative = np.where(unit_diag > 0, inverse_gap.sum(axis=1)[:, None], derivative)
    along_i = np.kron(derivative, np.eye(4))
    along_j = np.kron(np.eye(4), derivative)
    return (jnp.asarray(along_i, jnp.float32), jnp.asarray(along_j, jnp.float32))

def advance(element_grid, metric, rows_i, rows_j, start):
    first_term = jnp.einsum('an,flne->flae', rows_i, element_grid, precision=lax.Precision.HIGHEST)
    second_term = jnp.einsum('an,flne->flae', rows_j, element_grid, precision=lax.Precision.HIGHEST)
    return start + STEP_DYN * (metric[0] * first_term + metric[1] * second_term)

def radiate(tracers, sun_angle, kappa_base, band_kappa, solar_weight):
    squares = tracers * tracers
    groups = kappa_base.shape[0] // GBLOCK
    level_count = tracers.shape[1]
    column_count = tracers.shape[2]

    def one_group(running, pieces):
        base_rate, rate_rows, bright = pieces
        absorb = jnp.einsum('gt,tln->gln', rate_rows, squares, precision=lax.Precision.HIGHEST) + base_rate[:, None, None]
        layer_depth = absorb * DEPTH_UNIT
        depth_above = jnp.cumsum(layer_depth, axis=1) - layer_depth
        heating = jnp.einsum('g,gln->ln', bright, jnp.exp(-depth_above) * (1.0 - jnp.exp(-layer_depth)), precision=lax.Precision.HIGHEST)
        ground = jnp.einsum('g,gn->n', bright, jnp.exp(-(depth_above[:, -1] + layer_depth[:, -1])), precision=lax.Precision.HIGHEST)
        return ((running[0] + heating, running[1] + ground), None)
    start_vals = (jnp.zeros((level_count, column_count), jnp.float32), jnp.zeros((column_count,), jnp.float32))
    stacked = (kappa_base.reshape(groups, GBLOCK), band_kappa.reshape(groups, GBLOCK, -1), solar_weight.reshape(groups, GBLOCK))
    (heating, ground), _ = lax.scan(one_group, start_vals, stacked)
    sun_height = jnp.maximum(sun_angle, 0.0)
    return (HEAT_SCALE * sun_height * heating, FLUX_SCALE * sun_height * ground)

def reference(air_state, metric, jacobian, edge_nbr, edge_side, coszen, kappa_base, band_kappa, solar_weight, stretch_pos, stretch_src):
    field_count, level_count, all_cols = air_state.shape
    along_i, along_j = derivative_tables()
    element_grid = air_state.reshape(field_count, level_count, N_SFC, NODES, E_DEV).transpose(0, 1, 3, 2, 4).reshape(field_count, level_count, NODES, ELEMS)
    advanced = advance(element_grid, metric, along_i, along_j, element_grid)
    edge_flat = jnp.asarray(EDGE_NODES.reshape(-1))
    own_values = advanced[:, :, edge_flat]
    node_pick = jnp.asarray(EDGE_NODES[:, ::-1].copy())[edge_side]
    far_values = advanced[:, :, node_pick, edge_nbr[:, :, None]]
    far_values = far_values.transpose(0, 1, 2, 4, 3).reshape(field_count, level_count, 8, ELEMS)
    far_jac = jnp.broadcast_to(jacobian[edge_nbr][:, None, :], (4, 2, ELEMS)).reshape(8, ELEMS)
    summed = (jacobian * own_values + far_jac * far_values) / (jacobian + far_jac)
    dynamic = advanced.at[:, :, edge_flat].set(summed)
    dynamic = dynamic.reshape(field_count, level_count, NODES, N_SFC, E_DEV).transpose(0, 1, 3, 2, 4).reshape(field_count, level_count, all_cols)
    stretch_tracers = jnp.take(dynamic[4:], stretch_src, axis=2)
    stretch_sun = coszen[stretch_src]
    tracer_blocks = stretch_tracers.reshape(TRACERS, level_count, N_SFC, COLS_DEV).transpose(2, 0, 1, 3)
    sun_blocks = stretch_sun.reshape(N_SFC, COLS_DEV)

    def per_block(block_pair):
        return radiate(block_pair[0], block_pair[1], kappa_base, band_kappa, solar_weight)
    heating, ground = lax.map(per_block, (tracer_blocks, sun_blocks))
    heating = heating.transpose(1, 0, 2).reshape(level_count, all_cols)
    surface_flux = ground.reshape(-1)
    heat_cols = jnp.take(heating, stretch_pos, axis=1)
    new_state = dynamic.at[2].add(heat_cols)
    return (new_state, surface_flux)
```

```python
import functools

import jax
import jax.numpy as jnp
import numpy as np
from jax import lax
from jax.experimental import pallas as pl
from jax.experimental.pallas import tpu as pltpu
from jax.sharding import PartitionSpec as P

NODES = 16
GLL_POINTS = np.array([-1.0, -1.0 / np.sqrt(5.0), 1.0 / np.sqrt(5.0), 1.0])
EDGE_NODES = ((4, 8), (13, 14), (11, 7), (2, 1))
STEP_DYN = 0.2
DEPTH_UNIT = 0.05
HEAT_SCALE = 0.1
FLUX_SCALE = 0.02
F32 = jnp.float32
BF16 = jnp.bfloat16


def derivative_matrix():
    spacing = GLL_POINTS[:, None] - GLL_POINTS[None, :]
    unit_diag = np.eye(4)
    safe_space = np.where(unit_diag > 0, 1.0, spacing)
    weights_row = np.prod(safe_space, axis=1)
    derivative = weights_row[:, None] / weights_row[None, :] / safe_space
    inverse_gap = np.where(unit_diag > 0, 0.0, 1.0 / safe_space)
    return np.where(unit_diag > 0, inverse_gap.sum(axis=1)[:, None], derivative)


def split2(x):
    high = x.astype(BF16)
    return high, (x - high.astype(F32)).astype(BF16)


def dot(a, b):
    return jnp.dot(a, b, preferred_element_type=F32)


MESH = pl.DeviceIdType.MESH
EDGES = tuple(n for pair in EDGE_NODES for n in pair)
INNER = tuple(n for n in range(NODES) if n not in EDGES)


def column(row):
    n = row.shape[1]
    same = lax.broadcasted_iota(jnp.int32, (n, n), 0) == lax.broadcasted_iota(
        jnp.int32, (n, n), 1
    )
    return jnp.sum(jnp.where(same, jnp.broadcast_to(row, (n, n)), 0.0), axis=1, keepdims=True)


def log2(n):
    assert n & (n - 1) == 0
    return n.bit_length() - 1


def mix(a, b):
    return lax.dot_general(a, b, (((0,), (0,)), ((), ())), preferred_element_type=F32)


def spread_rates(bands, rows, per):
    high, low = split2(-DEPTH_UNIT * bands)
    shape = (bands.shape[0], 3 * rows)
    tracer = lax.broadcasted_iota(jnp.int32, shape, 0)
    lane = lax.broadcasted_iota(jnp.int32, shape, 1)
    third = jnp.where(lane >= rows, 1, 0) + jnp.where(lane >= 2 * rows, 1, 0)
    hit = (lane - third * rows) >> log2(per) == tracer
    one = lambda m: jnp.where(m, 1.0, 0.0).astype(BF16)
    return mix(high, one(hit & (third < 2))) + mix(low, one(hit & (third == 2)))


def stack3(x):
    high = x.astype(BF16).astype(F32)
    return jnp.concatenate([high, x - high, high], axis=0).astype(BF16)


def step_kernel(
    count,
    levels,
    chunks,
    state_ref,
    metric_hbm,
    jac_hbm,
    nbr_hbm,
    side_hbm,
    sun_hbm,
    base_hbm,
    band_hbm,
    weight_hbm,
    src_hbm,
    pos_hbm,
    new_ref,
    table_ref,
    index_ref,
    x_ref,
    seconds,
    firsts,
    direct_buf,
    relay_buf,
    cross_buf,
    mixed,
    mixed_buf,
    far0,
    far1,
    merged,
    choices,
    glow,
    heats,
    sq_inner,
    other_inner,
    sq_edge,
    other_edge,
    metric_ref,
    jac_ref,
    nbr_ref,
    side_ref,
    sun_ref,
    base_ref,
    band_ref,
    weight_ref,
    src_ref,
    pos_ref,
    their_nbr,
    their_side,
    direct_jac,
    relay_jac,
    spots,
    outbox,
    inbox,
    edge_send,
    edge_recv,
    meta_send,
    meta_recv,
    swap_send,
    swap_recv,
    flux_send,
    flux_recv,
    in_sem,
    small_sem,
):
    rows, cols = x_ref.shape
    ne = cols // NODES
    fields = rows // levels
    tracers = band_ref.shape[0]
    skip = rows - tracers * levels
    width = 4 * ne
    me, lev = lax.axis_index("sfc"), lax.axis_index("lev")
    odd = lax.rem(me, 2)
    partner = me + 1 - 2 * odd
    onward = lax.rem(me + count + 2 - 4 * odd, count)
    backward = lax.rem(me + count - 2 + 4 * odd, count)
    barrier = pltpu.get_barrier_semaphore()

    def greet(step, carry):
        pl.semaphore_signal(
            barrier, inc=1, device_id=(lax.rem(me + step, count), lev), device_id_type=MESH
        )
        return carry

    lax.fori_loop(1, count, greet, 0)
    pl.semaphore_signal(barrier, inc=1, device_id=(me, 1 - lev), device_id_type=MESH)

    small = [
        pltpu.make_async_copy(a, b, small_sem.at[i])
        for i, (a, b) in enumerate(
            (
                (metric_hbm, metric_ref),
                (jac_hbm, jac_ref),
                (nbr_hbm, nbr_ref),
                (side_hbm, side_ref),
                (band_hbm, band_ref),
                (base_hbm, base_ref),
                (weight_hbm, weight_ref),
                (sun_hbm, sun_ref),
                (pos_hbm, pos_ref),
                (src_hbm, src_ref),
            )
        )
    ]

    def fetch(f):
        return pltpu.make_async_copy(
            state_ref.at[f], x_ref.at[f * levels : (f + 1) * levels], in_sem.at[f]
        )

    for copy in small[:2]:
        copy.start()
    for start, stop in chunks:
        for f in range(start // levels, stop // levels):
            fetch(f).start()
        if start == chunks[0][0]:
            for copy in small[2:]:
                copy.start()

    d = derivative_matrix()

    def remote(src, dst, send, recv, to):
        return pltpu.make_async_remote_copy(
            src, dst, send, recv, device_id=to, device_id_type=MESH
        )

    def edge_copy(kind, src, dst, to):
        def make(c):
            part = slice(*chunks[c])
            return remote(
                src.at[part], dst.at[part], edge_send.at[kind, c], edge_recv.at[kind, c], (to, lev)
            )

        return make

    direct = edge_copy(0, seconds, direct_buf, partner)
    relay = edge_copy(1, direct_buf, relay_buf, onward)
    cross = edge_copy(2, firsts, cross_buf, backward)
    blend = edge_copy(3, mixed, mixed_buf, partner)
    meta = [
        remote(a, b, meta_send.at[i], meta_recv.at[i], (to, lev))
        for i, (a, b, to) in enumerate(
            (
                (jac_ref, direct_jac, partner),
                (direct_jac, relay_jac, onward),
                (nbr_hbm, their_nbr, partner),
                (side_hbm, their_side, partner),
            )
        )
    ]

    small[0].wait()
    small[1].wait()
    m0 = jnp.broadcast_to(STEP_DYN * metric_ref[0:1, :], (8, ne))
    m1 = jnp.broadcast_to(STEP_DYN * metric_ref[1:2, :], (8, ne))

    def advance(r, carry):
        sl = pl.ds(pl.multiple_of(r * 8, 8), 8)
        x = [x_ref[sl, n * ne : (n + 1) * ne] for n in range(NODES)]
        out = []
        for i in range(4):
            for j in range(4):
                one = sum(float(d[i, a]) * x[4 * a + j] for a in range(4))
                two = sum(float(d[j, a]) * x[4 * i + a] for a in range(4))
                out.append(x[4 * i + j] + (m0 * one + m1 * two))
        for n in INNER:
            new_ref[sl, n * ne : (n + 1) * ne] = out[n]
        for k, (a, b) in enumerate(EDGE_NODES):
            seconds[sl, k * ne : (k + 1) * ne] = out[b]
            firsts[sl, k * ne : (k + 1) * ne] = out[a]
        return carry

    last = len(chunks) - 1
    for c, (start, stop) in enumerate(chunks):
        for f in range(start // levels, stop // levels):
            fetch(f).wait()
        lax.fori_loop(start // 8, stop // 8, advance, 0)
        if c == 0:
            pl.semaphore_wait(barrier, count)
            for i in (0, 2, 3):
                meta[i].start()
        direct(c).start()
        if c < last:
            cross(c).start()

    def swap(part, a, b):
        return remote(a, b, swap_send.at[part], swap_recv.at[part], (me, 1 - lev))

    thick = tracers * levels
    padded = other_inner.shape[0]
    row = lax.broadcasted_iota(jnp.int32, (padded, 3 * thick), 0)
    lane = lax.broadcasted_iota(jnp.int32, (padded, 3 * thick), 1)
    lane = jnp.where(lane >= thick, lane - thick, lane)
    level_sum = jnp.where(lane >> log2(levels) == row, 1.0, 0.0).astype(BF16)

    def inner_tracers(part):
        nodes = INNER[part * 4 : part * 4 + 4]
        return jnp.concatenate(
            [new_ref[skip:, n * ne : (n + 1) * ne] for n in nodes], axis=1
        )

    for part in range(2):
        values = inner_tracers(part)
        sq_inner[:, part * width : (part + 1) * width] = dot(
            level_sum, stack3(values * values)
        )
    inner_swap = swap(0, sq_inner, other_inner)
    inner_swap.start()
    edge_swaps = [swap(1 + p, sq_edge.at[p], other_edge.at[p]) for p in range(2)]

    for copy in small[2:]:
        copy.wait()
    top = jnp.where(lev == 0, 1.0, 0.0).astype(F32)
    rates = spread_rates(band_ref[...], thick, levels)
    own_level = lax.rem(lax.broadcasted_iota(jnp.int32, rates.shape, 1), levels)
    own_rates = [jnp.where(own_level <= l, rates, 0.0).astype(BF16) for l in range(levels)]
    sum_rates = spread_rates(band_ref[...], padded, 1).astype(BF16)
    base = -DEPTH_UNIT * column(base_ref[...])
    weight = column(weight_ref[...])

    total_nodes = count * ne

    def spot_of(nbr, side, where):
        near = nbr - (where - 1) * ne
        near = jnp.where(near < 0, near + total_nodes, near)
        near = jnp.where(near >= total_nodes, near - total_nodes, near)
        window = jnp.where(near >= ne, 1, 0) + jnp.where(near >= 2 * ne, 1, 0)
        spot = window * (width - ne) + side * ne + near
        return jnp.concatenate([spot[k : k + 1, :] for k in range(4)], axis=1)

    def choose(i, target, w):
        lanes = lax.broadcasted_iota(jnp.int32, (width, width), 0) + w * width
        choices[i] = jnp.where(lanes == target, 1.0, 0.0).astype(BF16)

    def pick(values, i):
        n = values.shape[0]
        high, low = split2(values)
        both = dot(jnp.concatenate([high, low], axis=0), choices[i])
        return both[:n] + both[n:]

    def pick_jac(ref, i):
        wide = jnp.concatenate([jnp.broadcast_to(ref[...], (16, ne))] * 4, axis=1)
        return pick(wide, i)[0:1]

    def own_glow(slot, stacked):
        for l in range(levels):
            depth = dot(own_rates[l], stacked) + (l + 1.0) * base
            glow[slot, l] = weight * jnp.exp(depth)

    def finish(slot, other, sun):
        far = jnp.exp(dot(sum_rates, stack3(other)) + levels * base)
        keep = top + (1.0 - top) * far
        total = lambda v: jnp.sum(v, axis=0, keepdims=True)
        above = total(weight * keep)
        heat = []
        for l in range(levels):
            below = total(glow[slot, l] * keep)
            heat.append(HEAT_SCALE * sun * (above - below))
            above = below
        ground = FLUX_SCALE * sun * total(glow[slot, levels - 1] * far)
        return jnp.concatenate(heat, axis=0), ground

    def join(ref, row, nodes):
        return jnp.concatenate(
            [ref[row : row + 1, n * ne : (n + 1) * ne] for n in nodes], axis=1
        )

    lines = table_ref.shape[0]
    per = lines // count
    shift = log2(cols)

    def runs(device, place):
        ids = lax.broadcasted_iota(jnp.int32, (count, cols), 0)
        match = ids == device
        place = place.astype(F32)
        least = jnp.min(jnp.where(match, place, 1e9), axis=1, keepdims=True)
        return (place - jnp.sum(jnp.where(match, least, 0.0), axis=0, keepdims=True)).astype(
            jnp.int32
        )

    goes = pos_ref[...] >> shift
    rank = runs(goes, pos_ref[...])
    spots[0:1, :] = goes * per + (rank >> 7)
    spots[1:2, :] = rank & 127
    comes = src_ref[...] >> shift
    rank = runs(comes, lax.broadcasted_iota(jnp.int32, (1, cols), 1))
    spots[2:3, :] = comes * (per * 128) + rank
    taken = index_ref.shape[1]
    index_ref[...] = spots[2:3, pl.ds(pl.multiple_of(lev * taken, 128), taken)]

    def scatter(ground, nodes):
        line, lane = join(spots, 0, nodes), join(spots, 1, nodes)
        n = line.shape[1]
        there = lax.broadcasted_iota(jnp.int32, (lines, n), 0) == line
        high, _ = split2(ground)
        low, tail = split2(ground - high.astype(F32))
        parts = [jnp.where(there, v.astype(F32), 0.0) for v in (high, low, tail)]
        onehot = jnp.where(
            lax.broadcasted_iota(jnp.int32, (128, n), 0) == lane, 1.0, 0.0
        ).astype(BF16)
        out = lax.dot_general(
            jnp.concatenate(parts, axis=0).astype(BF16),
            onehot,
            (((1,), (1,)), ((), ())),
            preferred_element_type=F32,
        )
        return out[:lines] + out[lines : 2 * lines] + out[2 * lines :]

    def inner_part(part):
        nodes = INNER[part * 4 : part * 4 + 4]
        values = inner_tracers(part)
        own_glow(part, stack3(values * values))
        other = other_inner[:, part * width : (part + 1) * width]
        heat, ground = finish(part, other, jnp.maximum(join(sun_ref, 0, nodes), 0.0))
        for s, n in enumerate(nodes):
            lanes = slice(n * ne, (n + 1) * ne)
            new_ref[2 * levels : 3 * levels, lanes] = (
                new_ref[2 * levels : 3 * levels, lanes] + heat[:, s * ne : (s + 1) * ne]
            )
        return scatter(ground, nodes)

    target = spot_of(nbr_ref[...], side_ref[...], me)
    choose(0, target, 1)
    far1[...] = pick(firsts[...], 0)
    far0[...] = pick(seconds[...], 0)
    own_jac = pick_jac(jac_ref, 0)
    inner_swap.wait_recv()
    table = inner_part(0)

    def forward(c):
        direct(c).wait_recv()
        relay(c).start()

    meta[0].wait_recv()
    meta[1].start()
    forward(0)
    forward(1)
    meta[2].wait_recv()
    meta[3].wait_recv()
    theirs = spot_of(their_nbr[...], their_side[...], partner)
    choose(1, theirs, 2 * odd)
    choose(2, theirs, 2 - 2 * odd)
    mixed[...] = pick(firsts[...], 1)

    def answer(c):
        part = slice(*chunks[c])
        cross(c).wait_recv()
        mixed[part] = mixed[part] + pick(cross_buf[part], 2)
        blend(c).start()

    for c in range(last):
        answer(c)
        if 2 + c < last:
            forward(2 + c)
    cross(last).start()
    forward(last)
    table = table + inner_part(1)

    choose(3, target, 2 - 2 * odd)
    choose(4, target, 2 * odd)
    for c in range(last):
        part = slice(*chunks[c])
        far0[part] = far0[part] + pick(direct_buf[part], 3)
    meta[1].wait_recv()
    far_jac = own_jac + pick_jac(direct_jac, 3) + pick_jac(relay_jac, 4)
    mine = jnp.concatenate([jac_ref[...]] * 4, axis=1)
    own_part, far_part = mine / (mine + far_jac), far_jac / (mine + far_jac)
    nodes_of = [[a for a, _ in EDGE_NODES], [b for _, b in EDGE_NODES]]

    def put(p, part, values):
        for k, n in enumerate(nodes_of[p]):
            new_ref[part, n * ne : (n + 1) * ne] = values[:, k * ne : (k + 1) * ne]

    def merge(p, c):
        part = slice(*chunks[c])
        if p == 0:
            relay(c).wait_recv()
            far, own = far0[part] + pick(relay_buf[part], 4), firsts[part]
        else:
            blend(c).wait_recv()
            far, own = far1[part] + mixed_buf[part], seconds[part]
        return own_part * own + far_part * far

    def settle(p, c):
        part = slice(*chunks[c])
        values = merge(p, c)
        merged[p, part] = values
        put(p, part, values)

    def share(p):
        values = merged[p, skip:]
        stacked = stack3(values * values)
        sq_edge[p] = dot(level_sum, stacked)
        edge_swaps[p].start()
        own_glow(p, stacked)

    def shine(p):
        edge_swaps[p].wait_recv()
        sun = jnp.maximum(join(sun_ref, 0, nodes_of[p]), 0.0)
        heats[p], ground = finish(p, other_edge[p], sun)
        return scatter(ground, nodes_of[p])

    for c in range(last // 2):
        settle(0, c)
    for c in range(last):
        settle(1, c)
    share(1)
    for c in range(last // 2, last):
        settle(0, c)
    share(0)
    table = table + shine(1)
    table = table + shine(0)
    for k in range(count):
        outbox[k] = table[k * per : (k + 1) * per]

    def send(step):
        to = lax.rem(me + step, count)
        return remote(
            outbox.at[to], inbox.at[me], flux_send.at[step], flux_recv.at[me], (to, lev)
        )

    def arrive(step):
        peer = lax.rem(me + step, count)
        return remote(
            outbox.at[peer], inbox.at[peer], flux_send.at[step], flux_recv.at[peer], (peer, lev)
        )

    def start_send(step, carry):
        send(step).start()
        return carry

    def finish_send(step, carry):
        send(step).wait_send()
        arrive(step).wait_recv()
        return carry

    lax.fori_loop(1, count, start_send, 0)
    inbox[me] = outbox[me]

    answer(last)
    part = slice(*chunks[last])
    far0[part] = far0[part] + pick(direct_buf[part], 3)
    for p in range(2):
        values = merge(p, last)
        warm = slice(2 * levels, 3 * levels)
        values = jnp.concatenate(
            [values[: 2 * levels], values[warm] + heats[p], values[3 * levels :]], axis=0
        )
        put(p, part, values)
    for copy in meta + [inner_swap] + edge_swaps:
        copy.wait_send()
    for c in range(last + 1):
        for kind in (direct, relay, cross, blend):
            kind(c).wait_send()
    lax.fori_loop(1, count, finish_send, 0)
    for k in range(count):
        table_ref[k * per : (k + 1) * per, :] = inbox[k]


def store_kernel(levels, state_ref, table_ref, index_ref, new_ref, flux_ref, sem):
    fields = state_ref.shape[0] // levels

    def store(f):
        return pltpu.make_async_copy(
            state_ref.at[f * levels : (f + 1) * levels], new_ref.at[f], sem.at[f]
        )

    for f in range(fields):
        store(f).start()
    taken = flux_ref.shape[1]
    lines = table_ref.shape[0]
    index = index_ref[...]
    here = lax.broadcasted_iota(jnp.int32, (lines, taken), 0) == index >> 7
    onehot = jnp.where(here, 1.0, 0.0).astype(BF16)
    mask = lax.broadcasted_iota(jnp.int32, (128, taken), 0) == (index & 127)
    values = table_ref[...].T
    high, _ = split2(values)
    low, tail = split2(values - high.astype(F32))
    picked = dot(high, onehot) + dot(low, onehot) + dot(tail, onehot)
    flux_ref[...] = jnp.sum(jnp.where(mask, picked, 0.0), axis=0, keepdims=True)
    for f in range(fields):
        store(f).wait()


def row_chunks(rows, skip):
    groups = (rows - skip) // 8
    edges = [skip + 8 * round(groups * share) for share in (0.0, 0.3, 0.6, 0.8, 1.0)]
    return tuple(zip(edges[:-1], edges[1:])) + ((0, skip),)


def local(
    air_state,
    metric,
    jacobian,
    edge_nbr,
    edge_side,
    coszen,
    kappa_base,
    band_kappa,
    solar_weight,
    stretch_pos,
    stretch_src,
):
    fields, levels, cols = air_state.shape
    ne = cols // NODES
    rows = fields * levels
    width = 4 * ne
    points, tracers = band_kappa.shape
    padded = -(-tracers // 8) * 8
    count = lax.axis_size("sfc")
    part = cols // lax.axis_size("lev")
    chunks = row_chunks(rows, rows - tracers * levels)
    per = max(2 * cols // count // 128, 1)
    anywhere = pl.BlockSpec(memory_space=pl.ANY)
    vmem = pl.BlockSpec(memory_space=pltpu.VMEM)
    V = pltpu.VMEM
    sems = lambda *shape: pltpu.SemaphoreType.DMA(shape)
    new, table, index = pl.pallas_call(
        functools.partial(step_kernel, count, levels, chunks),
        in_specs=[pl.BlockSpec(memory_space=pltpu.HBM)] * 11,
        out_specs=(vmem, vmem, vmem),
        out_shape=(
            pltpu.VMEM((rows, cols), F32),
            pltpu.VMEM((count * per, 128), F32),
            pltpu.VMEM((1, part), jnp.int32),
        ),
        scratch_shapes=[
            V((rows, cols), F32),
            *[V((rows, width), F32)] * 9,
            V((2, rows, width), F32),
            V((5, width, width), BF16),
            V((2, levels, points, width), F32),
            V((2, levels, width), F32),
            *[V((padded, 2 * width), F32)] * 2,
            *[V((2, padded, width), F32)] * 2,
            V((2, ne), F32),
            V((1, ne), F32),
            V((4, ne), jnp.int32),
            V((4, ne), jnp.int32),
            V((1, cols), F32),
            V((1, points), F32),
            V((tracers, points), F32),
            V((1, points), F32),
            V((1, cols), jnp.int32),
            V((1, cols), jnp.int32),
            V((4, ne), jnp.int32),
            V((4, ne), jnp.int32),
            V((1, ne), F32),
            V((1, ne), F32),
            V((8, cols), jnp.int32),
            V((count, per, 128), F32),
            V((count, per, 128), F32),
            sems(4, len(chunks)),
            sems(4, len(chunks)),
            sems(4),
            sems(4),
            sems(3),
            sems(3),
            sems(count),
            sems(count),
            sems(fields),
            sems(10),
        ],
        compiler_params=pltpu.CompilerParams(
            collective_id=0, has_side_effects=True, vmem_limit_bytes=40 * 1024 * 1024
        ),
        name="step",
    )(
        *(
            pltpu.with_memory_space_constraint(a, pltpu.HBM)
            for a in (
        air_state,
        metric,
        jacobian[None, :],
        edge_nbr,
        edge_side,
        coszen[None, :],
        kappa_base[None, :],
        band_kappa.T,
        solar_weight[None, :],
        stretch_src[None, :],
        stretch_pos[None, :],
            )
        )
    )
    new, flux = pl.pallas_call(
        functools.partial(store_kernel, levels),
        in_specs=[vmem] * 3,
        out_specs=(anywhere, vmem),
        out_shape=(
            jax.ShapeDtypeStruct(air_state.shape, F32),
            jax.ShapeDtypeStruct((1, part), F32),
        ),
        scratch_shapes=[sems(fields)],
        compiler_params=pltpu.CompilerParams(vmem_limit_bytes=8 * 1024 * 1024),
        name="store",
    )(new, table, index)
    return (new, flux.reshape(part))


def solution(mesh):
    return jax.shard_map(
        local,
        mesh=mesh,
        in_specs=(
            P(None, "lev", "sfc"),
            P(None, "sfc"),
            P("sfc"),
            P(None, "sfc"),
            P(None, "sfc"),
            P("sfc"),
            P(),
            P(),
            P(),
            P("sfc"),
            P("sfc"),
        ),
        out_specs=(P(None, "lev", "sfc"), P(("sfc", "lev"))),
        check_vma=False,
    )
```

```python
import functools

import jax
import jax.numpy as jnp
import numpy as np
from jax import lax
from jax.experimental import pallas as pl
from jax.experimental.pallas import tpu as pltpu
from jax.sharding import PartitionSpec as P

NODES = 16
GLL_POINTS = np.array([-1.0, -1.0 / np.sqrt(5.0), 1.0 / np.sqrt(5.0), 1.0])
EDGE_NODES = ((4, 8), (13, 14), (11, 7), (2, 1))
STEP_DYN = 0.2
DEPTH_UNIT = 0.05
HEAT_SCALE = 0.1
FLUX_SCALE = 0.02
F32 = jnp.float32
BF16 = jnp.bfloat16


def derivative_matrix():
    spacing = GLL_POINTS[:, None] - GLL_POINTS[None, :]
    unit_diag = np.eye(4)
    safe_space = np.where(unit_diag > 0, 1.0, spacing)
    weights_row = np.prod(safe_space, axis=1)
    derivative = weights_row[:, None] / weights_row[None, :] / safe_space
    inverse_gap = np.where(unit_diag > 0, 0.0, 1.0 / safe_space)
    return np.where(unit_diag > 0, inverse_gap.sum(axis=1)[:, None], derivative)


def split2(x):
    high = x.astype(BF16)
    return high, (x - high.astype(F32)).astype(BF16)


def dot(a, b):
    return jnp.dot(a, b, preferred_element_type=F32)


MESH = pl.DeviceIdType.MESH
EDGES = tuple(n for pair in EDGE_NODES for n in pair)
INNER = tuple(n for n in range(NODES) if n not in EDGES)


def column(row):
    n = row.shape[1]
    same = lax.broadcasted_iota(jnp.int32, (n, n), 0) == lax.broadcasted_iota(
        jnp.int32, (n, n), 1
    )
    return jnp.sum(jnp.where(same, jnp.broadcast_to(row, (n, n)), 0.0), axis=1, keepdims=True)


def log2(n):
    assert n & (n - 1) == 0
    return n.bit_length() - 1


def mix(a, b):
    return lax.dot_general(a, b, (((0,), (0,)), ((), ())), preferred_element_type=F32)


def spread_rates(bands, rows, per):
    high, low = split2(-DEPTH_UNIT * bands)
    shape = (bands.shape[0], 3 * rows)
    tracer = lax.broadcasted_iota(jnp.int32, shape, 0)
    lane = lax.broadcasted_iota(jnp.int32, shape, 1)
    third = jnp.where(lane >= rows, 1, 0) + jnp.where(lane >= 2 * rows, 1, 0)
    hit = (lane - third * rows) >> log2(per) == tracer
    one = lambda m: jnp.where(m, 1.0, 0.0).astype(BF16)
    return mix(high, one(hit & (third < 2))) + mix(low, one(hit & (third == 2)))


def stack3(x):
    high = x.astype(BF16).astype(F32)
    return jnp.concatenate([high, x - high, high], axis=0).astype(BF16)


def step_kernel(
    count,
    levels,
    chunks,
    state_ref,
    metric_hbm,
    jac_hbm,
    nbr_hbm,
    side_hbm,
    sun_hbm,
    base_hbm,
    band_hbm,
    weight_hbm,
    src_hbm,
    pos_hbm,
    new_ref,
    table_ref,
    index_ref,
    x_ref,
    seconds,
    firsts,
    direct_buf,
    relay_buf,
    cross_buf,
    mixed,
    mixed_buf,
    far0,
    far1,
    merged,
    choices,
    glow,
    heats,
    sq_inner,
    other_inner,
    sq_edge,
    other_edge,
    metric_ref,
    jac_ref,
    nbr_ref,
    side_ref,
    sun_ref,
    base_ref,
    band_ref,
    weight_ref,
    src_ref,
    pos_ref,
    their_nbr,
    their_side,
    direct_jac,
    relay_jac,
    spots,
    outbox,
    inbox,
    edge_send,
    edge_recv,
    meta_send,
    meta_recv,
    swap_send,
    swap_recv,
    flux_send,
    flux_recv,
    in_sem,
    small_sem,
):
    rows, cols = x_ref.shape
    ne = cols // NODES
    fields = rows // levels
    tracers = band_ref.shape[0]
    skip = rows - tracers * levels
    width = 4 * ne
    me, lev = lax.axis_index("sfc"), lax.axis_index("lev")
    odd = lax.rem(me, 2)
    partner = me + 1 - 2 * odd
    onward = lax.rem(me + count + 2 - 4 * odd, count)
    backward = lax.rem(me + count - 2 + 4 * odd, count)
    barrier = pltpu.get_barrier_semaphore()

    def greet(step, carry):
        pl.semaphore_signal(
            barrier, inc=1, device_id=(lax.rem(me + step, count), lev), device_id_type=MESH
        )
        return carry

    lax.fori_loop(1, count, greet, 0)
    pl.semaphore_signal(barrier, inc=1, device_id=(me, 1 - lev), device_id_type=MESH)

    small = [
        pltpu.make_async_copy(a, b, small_sem.at[i])
        for i, (a, b) in enumerate(
            (
                (metric_hbm, metric_ref),
                (jac_hbm, jac_ref),
                (nbr_hbm, nbr_ref),
                (side_hbm, side_ref),
                (band_hbm, band_ref),
                (base_hbm, base_ref),
                (weight_hbm, weight_ref),
                (sun_hbm, sun_ref),
                (pos_hbm, pos_ref),
                (src_hbm, src_ref),
            )
        )
    ]

    def fetch(f):
        return pltpu.make_async_copy(
            state_ref.at[f], x_ref.at[f * levels : (f + 1) * levels], in_sem.at[f]
        )

    for copy in small[:2]:
        copy.start()
    for start, stop in chunks:
        for f in range(start // levels, stop // levels):
            fetch(f).start()
        if start == chunks[0][0]:
            for copy in small[2:]:
                copy.start()

    d = derivative_matrix()

    def remote(src, dst, send, recv, to):
        return pltpu.make_async_remote_copy(
            src, dst, send, recv, device_id=to, device_id_type=MESH
        )

    def edge_copy(kind, src, dst, to):
        def make(c):
            part = slice(*chunks[c])
            return remote(
                src.at[part], dst.at[part], edge_send.at[kind, c], edge_recv.at[kind, c], (to, lev)
            )

        return make

    direct = edge_copy(0, seconds, direct_buf, partner)
    relay = edge_copy(1, direct_buf, relay_buf, onward)
    cross = edge_copy(2, firsts, cross_buf, backward)
    blend = edge_copy(3, mixed, mixed_buf, partner)
    meta = [
        remote(a, b, meta_send.at[i], meta_recv.at[i], (to, lev))
        for i, (a, b, to) in enumerate(
            (
                (jac_ref, direct_jac, partner),
                (direct_jac, relay_jac, onward),
                (nbr_hbm, their_nbr, partner),
                (side_hbm, their_side, partner),
            )
        )
    ]

    small[0].wait()
    small[1].wait()
    m0 = jnp.broadcast_to(STEP_DYN * metric_ref[0:1, :], (8, ne))
    m1 = jnp.broadcast_to(STEP_DYN * metric_ref[1:2, :], (8, ne))

    def advance(r, carry):
        sl = pl.ds(pl.multiple_of(r * 8, 8), 8)
        x = [x_ref[sl, n * ne : (n + 1) * ne] for n in range(NODES)]
        out = []
        for i in range(4):
            for j in range(4):
                one = sum(float(d[i, a]) * x[4 * a + j] for a in range(4))
                two = sum(float(d[j, a]) * x[4 * i + a] for a in range(4))
                out.append(x[4 * i + j] + (m0 * one + m1 * two))
        for n in INNER:
            new_ref[sl, n * ne : (n + 1) * ne] = out[n]
        for k, (a, b) in enumerate(EDGE_NODES):
            seconds[sl, k * ne : (k + 1) * ne] = out[b]
            firsts[sl, k * ne : (k + 1) * ne] = out[a]
        return carry

    last = len(chunks) - 1
    for c, (start, stop) in enumerate(chunks):
        for f in range(start // levels, stop // levels):
            fetch(f).wait()
        lax.fori_loop(start // 8, stop // 8, advance, 0)
        if c == 0:
            pl.semaphore_wait(barrier, count)
            for i in (0, 2, 3):
                meta[i].start()
        if c < last:
            direct(c).start()
            cross(c).start()

    def swap(part, a, b):
        return remote(a, b, swap_send.at[part], swap_recv.at[part], (me, 1 - lev))

    thick = tracers * levels
    padded = other_inner.shape[0]
    row = lax.broadcasted_iota(jnp.int32, (padded, 3 * thick), 0)
    lane = lax.broadcasted_iota(jnp.int32, (padded, 3 * thick), 1)
    lane = jnp.where(lane >= thick, lane - thick, lane)
    level_sum = jnp.where(lane >> log2(levels) == row, 1.0, 0.0).astype(BF16)

    def inner_tracers(part):
        nodes = INNER[part * 4 : part * 4 + 4]
        return jnp.concatenate(
            [new_ref[skip:, n * ne : (n + 1) * ne] for n in nodes], axis=1
        )

    for part in range(2):
        values = inner_tracers(part)
        sq_inner[:, part * width : (part + 1) * width] = dot(
            level_sum, stack3(values * values)
        )
    inner_swap = swap(0, sq_inner, other_inner)
    inner_swap.start()
    edge_swaps = [swap(1 + p, sq_edge.at[p], other_edge.at[p]) for p in range(2)]

    for copy in small[2:]:
        copy.wait()
    top = jnp.where(lev == 0, 1.0, 0.0).astype(F32)
    rates = spread_rates(band_ref[...], thick, levels)
    own_level = lax.rem(lax.broadcasted_iota(jnp.int32, rates.shape, 1), levels)
    own_rates = [jnp.where(own_level <= l, rates, 0.0).astype(BF16) for l in range(levels)]
    sum_rates = spread_rates(band_ref[...], padded, 1).astype(BF16)
    base = -DEPTH_UNIT * column(base_ref[...])
    weight = column(weight_ref[...])

    total_nodes = count * ne

    def spot_of(nbr, side, where):
        near = nbr - (where - 1) * ne
        near = jnp.where(near < 0, near + total_nodes, near)
        near = jnp.where(near >= total_nodes, near - total_nodes, near)
        window = jnp.where(near >= ne, 1, 0) + jnp.where(near >= 2 * ne, 1, 0)
        spot = window * (width - ne) + side * ne + near
        return jnp.concatenate([spot[k : k + 1, :] for k in range(4)], axis=1)

    def choose(i, target, w):
        lanes = lax.broadcasted_iota(jnp.int32, (width, width), 0) + w * width
        choices[i] = jnp.where(lanes == target, 1.0, 0.0).astype(BF16)

    def pick(values, i):
        n = values.shape[0]
        high, low = split2(values)
        both = dot(jnp.concatenate([high, low], axis=0), choices[i])
        return both[:n] + both[n:]

    def pick_jac(ref, i):
        wide = jnp.concatenate([jnp.broadcast_to(ref[...], (16, ne))] * 4, axis=1)
        return pick(wide, i)[0:1]

    def own_glow(slot, stacked):
        for l in range(levels):
            depth = dot(own_rates[l], stacked) + (l + 1.0) * base
            glow[slot, l] = weight * jnp.exp(depth)

    def finish(slot, other, sun):
        far = jnp.exp(dot(sum_rates, stack3(other)) + levels * base)
        keep = top + (1.0 - top) * far
        total = lambda v: jnp.sum(v, axis=0, keepdims=True)
        above = total(weight * keep)
        heat = []
        for l in range(levels):
            below = total(glow[slot, l] * keep)
            heat.append(HEAT_SCALE * sun * (above - below))
            above = below
        ground = FLUX_SCALE * sun * total(glow[slot, levels - 1] * far)
        return jnp.concatenate(heat, axis=0), ground

    def join(ref, row, nodes):
        return jnp.concatenate(
            [ref[row : row + 1, n * ne : (n + 1) * ne] for n in nodes], axis=1
        )

    lines = table_ref.shape[0]
    per = lines // count
    shift = log2(cols)

    def runs(device, place):
        ids = lax.broadcasted_iota(jnp.int32, (count, cols), 0)
        match = ids == device
        place = place.astype(F32)
        least = jnp.min(jnp.where(match, place, 1e9), axis=1, keepdims=True)
        return (place - jnp.sum(jnp.where(match, least, 0.0), axis=0, keepdims=True)).astype(
            jnp.int32
        )

    goes = pos_ref[...] >> shift
    rank = runs(goes, pos_ref[...])
    spots[0:1, :] = goes * per + (rank >> 7)
    spots[1:2, :] = rank & 127
    comes = src_ref[...] >> shift
    rank = runs(comes, lax.broadcasted_iota(jnp.int32, (1, cols), 1))
    spots[2:3, :] = comes * (per * 128) + rank
    taken = index_ref.shape[1]
    index_ref[...] = spots[2:3, pl.ds(pl.multiple_of(lev * taken, 128), taken)]

    def scatter(ground, nodes):
        line, lane = join(spots, 0, nodes), join(spots, 1, nodes)
        n = line.shape[1]
        there = lax.broadcasted_iota(jnp.int32, (lines, n), 0) == line
        high, _ = split2(ground)
        low, tail = split2(ground - high.astype(F32))
        parts = [jnp.where(there, v.astype(F32), 0.0) for v in (high, low, tail)]
        onehot = jnp.where(
            lax.broadcasted_iota(jnp.int32, (128, n), 0) == lane, 1.0, 0.0
        ).astype(BF16)
        out = lax.dot_general(
            jnp.concatenate(parts, axis=0).astype(BF16),
            onehot,
            (((1,), (1,)), ((), ())),
            preferred_element_type=F32,
        )
        return out[:lines] + out[lines : 2 * lines] + out[2 * lines :]

    def inner_part(part):
        nodes = INNER[part * 4 : part * 4 + 4]
        values = inner_tracers(part)
        own_glow(part, stack3(values * values))
        other = other_inner[:, part * width : (part + 1) * width]
        heat, ground = finish(part, other, jnp.maximum(join(sun_ref, 0, nodes), 0.0))
        for s, n in enumerate(nodes):
            lanes = slice(n * ne, (n + 1) * ne)
            new_ref[2 * levels : 3 * levels, lanes] = (
                new_ref[2 * levels : 3 * levels, lanes] + heat[:, s * ne : (s + 1) * ne]
            )
        return scatter(ground, nodes)

    target = spot_of(nbr_ref[...], side_ref[...], me)
    choose(0, target, 1)
    far1[...] = pick(firsts[...], 0)
    far0[...] = pick(seconds[...], 0)
    own_jac = pick_jac(jac_ref, 0)
    inner_swap.wait_recv()
    table = inner_part(0)

    def forward(c):
        direct(c).wait_recv()
        relay(c).start()

    meta[0].wait_recv()
    meta[1].start()
    forward(0)
    forward(1)
    meta[2].wait_recv()
    meta[3].wait_recv()
    theirs = spot_of(their_nbr[...], their_side[...], partner)
    choose(1, theirs, 2 * odd)
    choose(2, theirs, 2 - 2 * odd)
    mixed[...] = pick(firsts[...], 1)

    def answer(c):
        part = slice(*chunks[c])
        cross(c).wait_recv()
        mixed[part] = mixed[part] + pick(cross_buf[part], 2)
        blend(c).start()

    for c in range(last):
        answer(c)
        if 2 + c < last:
            forward(2 + c)
    direct(last).start()
    cross(last).start()
    table = table + inner_part(1)

    choose(3, target, 2 - 2 * odd)
    choose(4, target, 2 * odd)
    for c in range(last):
        part = slice(*chunks[c])
        far0[part] = far0[part] + pick(direct_buf[part], 3)
    meta[1].wait_recv()
    far_jac = own_jac + pick_jac(direct_jac, 3) + pick_jac(relay_jac, 4)
    mine = jnp.concatenate([jac_ref[...]] * 4, axis=1)
    own_part, far_part = mine / (mine + far_jac), far_jac / (mine + far_jac)
    nodes_of = [[a for a, _ in EDGE_NODES], [b for _, b in EDGE_NODES]]

    def put(p, part, values):
        for k, n in enumerate(nodes_of[p]):
            new_ref[part, n * ne : (n + 1) * ne] = values[:, k * ne : (k + 1) * ne]

    def merge(p, c):
        part = slice(*chunks[c])
        if p == 0:
            relay(c).wait_recv()
            far, own = far0[part] + pick(relay_buf[part], 4), firsts[part]
        else:
            blend(c).wait_recv()
            far, own = far1[part] + mixed_buf[part], seconds[part]
        return own_part * own + far_part * far

    def settle(p, c):
        part = slice(*chunks[c])
        values = merge(p, c)
        merged[p, part] = values
        put(p, part, values)

    def share(p):
        values = merged[p, skip:]
        stacked = stack3(values * values)
        sq_edge[p] = dot(level_sum, stacked)
        edge_swaps[p].start()
        own_glow(p, stacked)

    def shine(p):
        edge_swaps[p].wait_recv()
        sun = jnp.maximum(join(sun_ref, 0, nodes_of[p]), 0.0)
        heats[p], ground = finish(p, other_edge[p], sun)
        return scatter(ground, nodes_of[p])

    for c in range(last // 2):
        settle(0, c)
    for c in range(last):
        settle(1, c)
    share(1)
    for c in range(last // 2, last):
        settle(0, c)
    share(0)
    table = table + shine(1)
    table = table + shine(0)
    for k in range(count):
        outbox[k] = table[k * per : (k + 1) * per]

    def send(step):
        to = lax.rem(me + step, count)
        return remote(
            outbox.at[to], inbox.at[me], flux_send.at[step], flux_recv.at[me], (to, lev)
        )

    def arrive(step):
        peer = lax.rem(me + step, count)
        return remote(
            outbox.at[peer], inbox.at[peer], flux_send.at[step], flux_recv.at[peer], (peer, lev)
        )

    def start_send(step, carry):
        send(step).start()
        return carry

    def finish_send(step, carry):
        send(step).wait_send()
        arrive(step).wait_recv()
        return carry

    lax.fori_loop(1, count, start_send, 0)
    inbox[me] = outbox[me]

    answer(last)
    forward(last)
    part = slice(*chunks[last])
    far0[part] = far0[part] + pick(direct_buf[part], 3)
    for p in range(2):
        values = merge(p, last)
        warm = slice(2 * levels, 3 * levels)
        values = jnp.concatenate(
            [values[: 2 * levels], values[warm] + heats[p], values[3 * levels :]], axis=0
        )
        put(p, part, values)
    for copy in meta + [inner_swap] + edge_swaps:
        copy.wait_send()
    for c in range(last + 1):
        for kind in (direct, relay, cross, blend):
            kind(c).wait_send()
    lax.fori_loop(1, count, finish_send, 0)
    for k in range(count):
        table_ref[k * per : (k + 1) * per, :] = inbox[k]


def store_kernel(levels, state_ref, table_ref, index_ref, new_ref, flux_out, flux_ref, sem):
    fields = state_ref.shape[0] // levels

    def store(f):
        return pltpu.make_async_copy(
            state_ref.at[f * levels : (f + 1) * levels], new_ref.at[f], sem.at[f]
        )

    for f in range(fields):
        store(f).start()
    taken = flux_ref.shape[1]
    lines = table_ref.shape[0]
    index = index_ref[...]
    here = lax.broadcasted_iota(jnp.int32, (lines, taken), 0) == index >> 7
    onehot = jnp.where(here, 1.0, 0.0).astype(BF16)
    mask = lax.broadcasted_iota(jnp.int32, (128, taken), 0) == (index & 127)
    values = table_ref[...].T
    high, _ = split2(values)
    low, tail = split2(values - high.astype(F32))
    picked = dot(high, onehot) + dot(low, onehot) + dot(tail, onehot)
    flux_ref[...] = jnp.sum(jnp.where(mask, picked, 0.0), axis=0, keepdims=True)
    give = pltpu.make_async_copy(flux_ref, flux_out, sem.at[fields])
    give.start()
    for f in range(fields):
        store(f).wait()
    give.wait()


def row_chunks(rows, skip):
    groups = (rows - skip) // 8
    edges = [skip + 8 * round(groups * share) for share in (0.0, 0.2, 0.5, 0.8, 1.0)]
    return tuple(zip(edges[:-1], edges[1:])) + ((0, skip),)


def local(
    air_state,
    metric,
    jacobian,
    edge_nbr,
    edge_side,
    coszen,
    kappa_base,
    band_kappa,
    solar_weight,
    stretch_pos,
    stretch_src,
):
    fields, levels, cols = air_state.shape
    ne = cols // NODES
    rows = fields * levels
    width = 4 * ne
    points, tracers = band_kappa.shape
    padded = -(-tracers // 8) * 8
    count = lax.axis_size("sfc")
    part = cols // lax.axis_size("lev")
    chunks = row_chunks(rows, rows - tracers * levels)
    per = max(2 * cols // count // 128, 1)
    anywhere = pl.BlockSpec(memory_space=pl.ANY)
    vmem = pl.BlockSpec(memory_space=pltpu.VMEM)
    V = pltpu.VMEM
    sems = lambda *shape: pltpu.SemaphoreType.DMA(shape)
    new, table, index = pl.pallas_call(
        functools.partial(step_kernel, count, levels, chunks),
        in_specs=[pl.BlockSpec(memory_space=pltpu.HBM)] * 11,
        out_specs=(vmem, vmem, vmem),
        out_shape=(
            pltpu.VMEM((rows, cols), F32),
            pltpu.VMEM((count * per, 128), F32),
            pltpu.VMEM((1, part), jnp.int32),
        ),
        scratch_shapes=[
            V((rows, cols), F32),
            *[V((rows, width), F32)] * 9,
            V((2, rows, width), F32),
            V((5, width, width), BF16),
            V((2, levels, points, width), F32),
            V((2, levels, width), F32),
            *[V((padded, 2 * width), F32)] * 2,
            *[V((2, padded, width), F32)] * 2,
            V((2, ne), F32),
            V((1, ne), F32),
            V((4, ne), jnp.int32),
            V((4, ne), jnp.int32),
            V((1, cols), F32),
            V((1, points), F32),
            V((tracers, points), F32),
            V((1, points), F32),
            V((1, cols), jnp.int32),
            V((1, cols), jnp.int32),
            V((4, ne), jnp.int32),
            V((4, ne), jnp.int32),
            V((1, ne), F32),
            V((1, ne), F32),
            V((8, cols), jnp.int32),
            V((count, per, 128), F32),
            V((count, per, 128), F32),
            sems(4, len(chunks)),
            sems(4, len(chunks)),
            sems(4),
            sems(4),
            sems(3),
            sems(3),
            sems(count),
            sems(count),
            sems(fields),
            sems(10),
        ],
        compiler_params=pltpu.CompilerParams(
            collective_id=0, has_side_effects=True, vmem_limit_bytes=40 * 1024 * 1024
        ),
        name="step",
    )(
        *(
            pltpu.with_memory_space_constraint(a, pltpu.HBM)
            for a in (
        air_state,
        metric,
        jacobian[None, :],
        edge_nbr,
        edge_side,
        coszen[None, :],
        kappa_base[None, :],
        band_kappa.T,
        solar_weight[None, :],
        stretch_src[None, :],
        stretch_pos[None, :],
            )
        )
    )
    new, flux = pl.pallas_call(
        functools.partial(store_kernel, levels),
        in_specs=[vmem] * 3,
        out_specs=(anywhere, anywhere),
        out_shape=(
            jax.ShapeDtypeStruct(air_state.shape, F32),
            jax.ShapeDtypeStruct((1, part), F32),
        ),
        scratch_shapes=[V((1, part), F32), sems(fields + 1)],
        compiler_params=pltpu.CompilerParams(vmem_limit_bytes=8 * 1024 * 1024),
        name="store",
    )(new, table, index)
    return (new, flux.reshape(part))


def solution(mesh):
    return jax.shard_map(
        local,
        mesh=mesh,
        in_specs=(
            P(None, "lev", "sfc"),
            P(None, "sfc"),
            P("sfc"),
            P(None, "sfc"),
            P(None, "sfc"),
            P("sfc"),
            P(),
            P(),
            P(),
            P("sfc"),
            P("sfc"),
        ),
        out_specs=(P(None, "lev", "sfc"), P(("sfc", "lev"))),
        check_vma=False,
    )
```

```python
import functools

import jax
import jax.numpy as jnp
import numpy as np
from jax import lax
from jax.experimental import pallas as pl
from jax.experimental.pallas import tpu as pltpu
from jax.sharding import PartitionSpec as P

NODES = 16
GLL_POINTS = np.array([-1.0, -1.0 / np.sqrt(5.0), 1.0 / np.sqrt(5.0), 1.0])
EDGE_NODES = ((4, 8), (13, 14), (11, 7), (2, 1))
STEP_DYN = 0.2
DEPTH_UNIT = 0.05
HEAT_SCALE = 0.1
FLUX_SCALE = 0.02
F32 = jnp.float32
BF16 = jnp.bfloat16


def derivative_matrix():
    spacing = GLL_POINTS[:, None] - GLL_POINTS[None, :]
    unit_diag = np.eye(4)
    safe_space = np.where(unit_diag > 0, 1.0, spacing)
    weights_row = np.prod(safe_space, axis=1)
    derivative = weights_row[:, None] / weights_row[None, :] / safe_space
    inverse_gap = np.where(unit_diag > 0, 0.0, 1.0 / safe_space)
    return np.where(unit_diag > 0, inverse_gap.sum(axis=1)[:, None], derivative)


def split2(x):
    high = x.astype(BF16)
    return high, (x - high.astype(F32)).astype(BF16)


def dot(a, b):
    return jnp.dot(a, b, preferred_element_type=F32)


MESH = pl.DeviceIdType.MESH
EDGES = tuple(n for pair in EDGE_NODES for n in pair)
INNER = tuple(n for n in range(NODES) if n not in EDGES)


def column(row):
    n = row.shape[1]
    same = lax.broadcasted_iota(jnp.int32, (n, n), 0) == lax.broadcasted_iota(
        jnp.int32, (n, n), 1
    )
    return jnp.sum(jnp.where(same, jnp.broadcast_to(row, (n, n)), 0.0), axis=1, keepdims=True)


def log2(n):
    assert n & (n - 1) == 0
    return n.bit_length() - 1


def mix(a, b):
    return lax.dot_general(a, b, (((0,), (0,)), ((), ())), preferred_element_type=F32)


def spread_rates(bands, rows, per):
    high, low = split2(-DEPTH_UNIT * bands)
    shape = (bands.shape[0], 3 * rows)
    tracer = lax.broadcasted_iota(jnp.int32, shape, 0)
    lane = lax.broadcasted_iota(jnp.int32, shape, 1)
    third = jnp.where(lane >= rows, 1, 0) + jnp.where(lane >= 2 * rows, 1, 0)
    hit = (lane - third * rows) >> log2(per) == tracer
    one = lambda m: jnp.where(m, 1.0, 0.0).astype(BF16)
    return mix(high, one(hit & (third < 2))) + mix(low, one(hit & (third == 2)))


def stack3(x):
    high = x.astype(BF16).astype(F32)
    return jnp.concatenate([high, x - high, high], axis=0).astype(BF16)


def step_kernel(
    count,
    levels,
    chunks,
    state_ref,
    metric_hbm,
    jac_hbm,
    nbr_hbm,
    side_hbm,
    sun_hbm,
    base_hbm,
    band_hbm,
    weight_hbm,
    src_hbm,
    pos_hbm,
    new_ref,
    table_ref,
    index_ref,
    x_ref,
    seconds,
    firsts,
    direct_buf,
    relay_buf,
    cross_buf,
    mixed,
    mixed_buf,
    far0,
    far1,
    merged,
    choices,
    glow,
    heats,
    sq_inner,
    other_inner,
    sq_edge,
    other_edge,
    metric_ref,
    jac_ref,
    nbr_ref,
    side_ref,
    sun_ref,
    base_ref,
    band_ref,
    weight_ref,
    src_ref,
    pos_ref,
    their_nbr,
    their_side,
    direct_jac,
    relay_jac,
    spots,
    outbox,
    inbox,
    edge_send,
    edge_recv,
    meta_send,
    meta_recv,
    swap_send,
    swap_recv,
    flux_send,
    flux_recv,
    in_sem,
    small_sem,
):
    rows, cols = x_ref.shape
    ne = cols // NODES
    fields = rows // levels
    tracers = band_ref.shape[0]
    skip = rows - tracers * levels
    width = 4 * ne
    me, lev = lax.axis_index("sfc"), lax.axis_index("lev")
    odd = lax.rem(me, 2)
    partner = me + 1 - 2 * odd
    onward = lax.rem(me + count + 2 - 4 * odd, count)
    backward = lax.rem(me + count - 2 + 4 * odd, count)
    barrier = pltpu.get_barrier_semaphore()

    def greet(step, carry):
        pl.semaphore_signal(
            barrier, inc=1, device_id=(lax.rem(me + step, count), lev), device_id_type=MESH
        )
        return carry

    lax.fori_loop(1, count, greet, 0)
    pl.semaphore_signal(barrier, inc=1, device_id=(me, 1 - lev), device_id_type=MESH)

    small = [
        pltpu.make_async_copy(a, b, small_sem.at[i])
        for i, (a, b) in enumerate(
            (
                (metric_hbm, metric_ref),
                (jac_hbm, jac_ref),
                (nbr_hbm, nbr_ref),
                (side_hbm, side_ref),
                (band_hbm, band_ref),
                (base_hbm, base_ref),
                (weight_hbm, weight_ref),
                (sun_hbm, sun_ref),
                (pos_hbm, pos_ref),
                (src_hbm, src_ref),
            )
        )
    ]

    def fetch(f):
        return pltpu.make_async_copy(
            state_ref.at[f], x_ref.at[f * levels : (f + 1) * levels], in_sem.at[f]
        )

    for copy in small[:2]:
        copy.start()
    for start, stop in chunks:
        for f in range(start // levels, stop // levels):
            fetch(f).start()
        if start == chunks[0][0]:
            for copy in small[2:]:
                copy.start()

    d = derivative_matrix()

    def remote(src, dst, send, recv, to):
        return pltpu.make_async_remote_copy(
            src, dst, send, recv, device_id=to, device_id_type=MESH
        )

    def edge_copy(kind, src, dst, to):
        def make(c):
            part = slice(*chunks[c])
            return remote(
                src.at[part], dst.at[part], edge_send.at[kind, c], edge_recv.at[kind, c], (to, lev)
            )

        return make

    direct = edge_copy(0, seconds, direct_buf, partner)
    relay = edge_copy(1, direct_buf, relay_buf, onward)
    cross = edge_copy(2, firsts, cross_buf, backward)
    blend = edge_copy(3, mixed, mixed_buf, partner)
    meta = [
        remote(a, b, meta_send.at[i], meta_recv.at[i], (to, lev))
        for i, (a, b, to) in enumerate(
            (
                (jac_ref, direct_jac, partner),
                (direct_jac, relay_jac, onward),
                (nbr_hbm, their_nbr, partner),
                (side_hbm, their_side, partner),
            )
        )
    ]

    small[0].wait()
    small[1].wait()
    m0 = jnp.broadcast_to(STEP_DYN * metric_ref[0:1, :], (8, ne))
    m1 = jnp.broadcast_to(STEP_DYN * metric_ref[1:2, :], (8, ne))

    def advance(r, carry):
        sl = pl.ds(pl.multiple_of(r * 8, 8), 8)
        x = [x_ref[sl, n * ne : (n + 1) * ne] for n in range(NODES)]
        out = []
        for i in range(4):
            for j in range(4):
                one = sum(float(d[i, a]) * x[4 * a + j] for a in range(4))
                two = sum(float(d[j, a]) * x[4 * i + a] for a in range(4))
                out.append(x[4 * i + j] + (m0 * one + m1 * two))
        for n in INNER:
            new_ref[sl, n * ne : (n + 1) * ne] = out[n]
        for k, (a, b) in enumerate(EDGE_NODES):
            seconds[sl, k * ne : (k + 1) * ne] = out[b]
            firsts[sl, k * ne : (k + 1) * ne] = out[a]
        return carry

    last = len(chunks) - 1
    for c, (start, stop) in enumerate(chunks):
        for f in range(start // levels, stop // levels):
            fetch(f).wait()
        lax.fori_loop(start // 8, stop // 8, advance, 0)
        if c == 0:
            pl.semaphore_wait(barrier, count)
            for i in (0, 2, 3):
                meta[i].start()
        direct(c).start()
        cross(c).start()

    def swap(part, a, b):
        return remote(a, b, swap_send.at[part], swap_recv.at[part], (me, 1 - lev))

    thick = tracers * levels
    padded = other_inner.shape[0]
    row = lax.broadcasted_iota(jnp.int32, (padded, 3 * thick), 0)
    lane = lax.broadcasted_iota(jnp.int32, (padded, 3 * thick), 1)
    lane = jnp.where(lane >= thick, lane - thick, lane)
    level_sum = jnp.where(lane >> log2(levels) == row, 1.0, 0.0).astype(BF16)

    def inner_tracers(part):
        nodes = INNER[part * 4 : part * 4 + 4]
        return jnp.concatenate(
            [new_ref[skip:, n * ne : (n + 1) * ne] for n in nodes], axis=1
        )

    for part in range(2):
        values = inner_tracers(part)
        sq_inner[:, part * width : (part + 1) * width] = dot(
            level_sum, stack3(values * values)
        )
    inner_swap = swap(0, sq_inner, other_inner)
    inner_swap.start()
    edge_swaps = [swap(1 + p, sq_edge.at[p], other_edge.at[p]) for p in range(2)]

    for copy in small[2:]:
        copy.wait()
    top = jnp.where(lev == 0, 1.0, 0.0).astype(F32)
    rates = spread_rates(band_ref[...], thick, levels)
    own_level = lax.rem(lax.broadcasted_iota(jnp.int32, rates.shape, 1), levels)
    own_rates = [jnp.where(own_level <= l, rates, 0.0).astype(BF16) for l in range(levels)]
    sum_rates = spread_rates(band_ref[...], padded, 1).astype(BF16)
    base = -DEPTH_UNIT * column(base_ref[...])
    weight = column(weight_ref[...])

    total_nodes = count * ne

    def spot_of(nbr, side, where):
        near = nbr - (where - 1) * ne
        near = jnp.where(near < 0, near + total_nodes, near)
        near = jnp.where(near >= total_nodes, near - total_nodes, near)
        window = jnp.where(near >= ne, 1, 0) + jnp.where(near >= 2 * ne, 1, 0)
        spot = window * (width - ne) + side * ne + near
        return jnp.concatenate([spot[k : k + 1, :] for k in range(4)], axis=1)

    def choose(i, target, w):
        lanes = lax.broadcasted_iota(jnp.int32, (width, width), 0) + w * width
        choices[i] = jnp.where(lanes == target, 1.0, 0.0).astype(BF16)

    def pick(values, i):
        n = values.shape[0]
        high, low = split2(values)
        both = dot(jnp.concatenate([high, low], axis=0), choices[i])
        return both[:n] + both[n:]

    def pick_jac(ref, i):
        wide = jnp.concatenate([jnp.broadcast_to(ref[...], (16, ne))] * 4, axis=1)
        return pick(wide, i)[0:1]

    def own_glow(slot, stacked):
        for l in range(levels):
            depth = dot(own_rates[l], stacked) + (l + 1.0) * base
            glow[slot, l] = weight * jnp.exp(depth)

    def finish(slot, other, sun):
        far = jnp.exp(dot(sum_rates, stack3(other)) + levels * base)
        keep = top + (1.0 - top) * far
        total = lambda v: jnp.sum(v, axis=0, keepdims=True)
        above = total(weight * keep)
        heat = []
        for l in range(levels):
            below = total(glow[slot, l] * keep)
            heat.append(HEAT_SCALE * sun * (above - below))
            above = below
        ground = FLUX_SCALE * sun * total(glow[slot, levels - 1] * far)
        return jnp.concatenate(heat, axis=0), ground

    def join(ref, row, nodes):
        return jnp.concatenate(
            [ref[row : row + 1, n * ne : (n + 1) * ne] for n in nodes], axis=1
        )

    lines = table_ref.shape[0]
    per = lines // count
    shift = log2(cols)

    def runs(device, place):
        ids = lax.broadcasted_iota(jnp.int32, (count, cols), 0)
        match = ids == device
        place = place.astype(F32)
        least = jnp.min(jnp.where(match, place, 1e9), axis=1, keepdims=True)
        return (place - jnp.sum(jnp.where(match, least, 0.0), axis=0, keepdims=True)).astype(
            jnp.int32
        )

    goes = pos_ref[...] >> shift
    rank = runs(goes, pos_ref[...])
    spots[0:1, :] = goes * per + (rank >> 7)
    spots[1:2, :] = rank & 127
    comes = src_ref[...] >> shift
    rank = runs(comes, lax.broadcasted_iota(jnp.int32, (1, cols), 1))
    spots[2:3, :] = comes * (per * 128) + rank
    taken = index_ref.shape[1]
    index_ref[...] = spots[2:3, pl.ds(pl.multiple_of(lev * taken, 128), taken)]

    def scatter(ground, nodes):
        line, lane = join(spots, 0, nodes), join(spots, 1, nodes)
        n = line.shape[1]
        there = lax.broadcasted_iota(jnp.int32, (lines, n), 0) == line
        high, _ = split2(ground)
        low, tail = split2(ground - high.astype(F32))
        parts = [jnp.where(there, v.astype(F32), 0.0) for v in (high, low, tail)]
        onehot = jnp.where(
            lax.broadcasted_iota(jnp.int32, (128, n), 0) == lane, 1.0, 0.0
        ).astype(BF16)
        out = lax.dot_general(
            jnp.concatenate(parts, axis=0).astype(BF16),
            onehot,
            (((1,), (1,)), ((), ())),
            preferred_element_type=F32,
        )
        return out[:lines] + out[lines : 2 * lines] + out[2 * lines :]

    def inner_part(part):
        nodes = INNER[part * 4 : part * 4 + 4]
        values = inner_tracers(part)
        own_glow(part, stack3(values * values))
        other = other_inner[:, part * width : (part + 1) * width]
        heat, ground = finish(part, other, jnp.maximum(join(sun_ref, 0, nodes), 0.0))
        for s, n in enumerate(nodes):
            lanes = slice(n * ne, (n + 1) * ne)
            new_ref[2 * levels : 3 * levels, lanes] = (
                new_ref[2 * levels : 3 * levels, lanes] + heat[:, s * ne : (s + 1) * ne]
            )
        return scatter(ground, nodes)

    target = spot_of(nbr_ref[...], side_ref[...], me)
    choose(0, target, 1)
    far1[...] = pick(firsts[...], 0)
    far0[...] = pick(seconds[...], 0)
    own_jac = pick_jac(jac_ref, 0)
    inner_swap.wait_recv()
    table = inner_part(0)

    def forward(c):
        direct(c).wait_recv()
        relay(c).start()

    meta[0].wait_recv()
    meta[1].start()
    forward(0)
    forward(1)
    meta[2].wait_recv()
    meta[3].wait_recv()
    theirs = spot_of(their_nbr[...], their_side[...], partner)
    choose(1, theirs, 2 * odd)
    choose(2, theirs, 2 - 2 * odd)
    mixed[...] = pick(firsts[...], 1)

    def answer(c):
        part = slice(*chunks[c])
        cross(c).wait_recv()
        mixed[part] = mixed[part] + pick(cross_buf[part], 2)
        blend(c).start()

    for c in range(last):
        answer(c)
        if 2 + c < last:
            forward(2 + c)
    forward(last)
    answer(last)
    table = table + inner_part(1)

    choose(3, target, 2 - 2 * odd)
    choose(4, target, 2 * odd)
    for c in range(last):
        part = slice(*chunks[c])
        far0[part] = far0[part] + pick(direct_buf[part], 3)
    meta[1].wait_recv()
    far_jac = own_jac + pick_jac(direct_jac, 3) + pick_jac(relay_jac, 4)
    mine = jnp.concatenate([jac_ref[...]] * 4, axis=1)
    own_part, far_part = mine / (mine + far_jac), far_jac / (mine + far_jac)
    nodes_of = [[a for a, _ in EDGE_NODES], [b for _, b in EDGE_NODES]]

    def put(p, part, values):
        for k, n in enumerate(nodes_of[p]):
            new_ref[part, n * ne : (n + 1) * ne] = values[:, k * ne : (k + 1) * ne]

    def merge(p, c):
        part = slice(*chunks[c])
        if p == 0:
            relay(c).wait_recv()
            far, own = far0[part] + pick(relay_buf[part], 4), firsts[part]
        else:
            blend(c).wait_recv()
            far, own = far1[part] + mixed_buf[part], seconds[part]
        return own_part * own + far_part * far

    def settle(p, c):
        part = slice(*chunks[c])
        values = merge(p, c)
        merged[p, part] = values
        put(p, part, values)

    def share(p):
        values = merged[p, skip:]
        stacked = stack3(values * values)
        sq_edge[p] = dot(level_sum, stacked)
        edge_swaps[p].start()
        own_glow(p, stacked)

    def shine(p):
        edge_swaps[p].wait_recv()
        sun = jnp.maximum(join(sun_ref, 0, nodes_of[p]), 0.0)
        heats[p], ground = finish(p, other_edge[p], sun)
        return scatter(ground, nodes_of[p])

    for c in range(last // 2):
        settle(0, c)
    for c in range(last):
        settle(1, c)
    share(1)
    for c in range(last // 2, last):
        settle(0, c)
    share(0)
    table = table + shine(1)
    table = table + shine(0)
    for k in range(count):
        outbox[k] = table[k * per : (k + 1) * per]

    def send(step):
        to = lax.rem(me + step, count)
        return remote(
            outbox.at[to], inbox.at[me], flux_send.at[step], flux_recv.at[me], (to, lev)
        )

    def arrive(step):
        peer = lax.rem(me + step, count)
        return remote(
            outbox.at[peer], inbox.at[peer], flux_send.at[step], flux_recv.at[peer], (peer, lev)
        )

    def start_send(step, carry):
        send(step).start()
        return carry

    def finish_send(step, carry):
        send(step).wait_send()
        arrive(step).wait_recv()
        return carry

    lax.fori_loop(1, count, start_send, 0)
    inbox[me] = outbox[me]

    part = slice(*chunks[last])
    far0[part] = far0[part] + pick(direct_buf[part], 3)
    for p in range(2):
        values = merge(p, last)
        warm = slice(2 * levels, 3 * levels)
        values = jnp.concatenate(
            [values[: 2 * levels], values[warm] + heats[p], values[3 * levels :]], axis=0
        )
        put(p, part, values)
    for copy in meta + [inner_swap] + edge_swaps:
        copy.wait_send()
    for c in range(last + 1):
        for kind in (direct, relay, cross, blend):
            kind(c).wait_send()
    lax.fori_loop(1, count, finish_send, 0)
    for k in range(count):
        table_ref[k * per : (k + 1) * per, :] = inbox[k]


def store_kernel(levels, state_ref, table_ref, index_ref, new_ref, flux_out, flux_ref, sem):
    fields = state_ref.shape[0] // levels

    def store(f):
        return pltpu.make_async_copy(
            state_ref.at[f * levels : (f + 1) * levels], new_ref.at[f], sem.at[f]
        )

    for f in range(fields):
        store(f).start()
    taken = flux_ref.shape[1]
    lines = table_ref.shape[0]
    index = index_ref[...]
    here = lax.broadcasted_iota(jnp.int32, (lines, taken), 0) == index >> 7
    onehot = jnp.where(here, 1.0, 0.0).astype(BF16)
    mask = lax.broadcasted_iota(jnp.int32, (128, taken), 0) == (index & 127)
    values = table_ref[...].T
    high, _ = split2(values)
    low, tail = split2(values - high.astype(F32))
    picked = dot(high, onehot) + dot(low, onehot) + dot(tail, onehot)
    flux_ref[...] = jnp.sum(jnp.where(mask, picked, 0.0), axis=0, keepdims=True)
    give = pltpu.make_async_copy(flux_ref, flux_out, sem.at[fields])
    give.start()
    for f in range(fields):
        store(f).wait()
    give.wait()


def row_chunks(rows, skip):
    groups = (rows - skip) // 8
    edges = [skip + 8 * round(groups * share) for share in (0.0, 0.2, 0.5, 0.8, 1.0)]
    return tuple(zip(edges[:-1], edges[1:])) + ((0, skip),)


def local(
    air_state,
    metric,
    jacobian,
    edge_nbr,
    edge_side,
    coszen,
    kappa_base,
    band_kappa,
    solar_weight,
    stretch_pos,
    stretch_src,
):
    fields, levels, cols = air_state.shape
    ne = cols // NODES
    rows = fields * levels
    width = 4 * ne
    points, tracers = band_kappa.shape
    padded = -(-tracers // 8) * 8
    count = lax.axis_size("sfc")
    part = cols // lax.axis_size("lev")
    chunks = row_chunks(rows, rows - tracers * levels)
    per = max(2 * cols // count // 128, 1)
    anywhere = pl.BlockSpec(memory_space=pl.ANY)
    vmem = pl.BlockSpec(memory_space=pltpu.VMEM)
    V = pltpu.VMEM
    sems = lambda *shape: pltpu.SemaphoreType.DMA(shape)
    new, table, index = pl.pallas_call(
        functools.partial(step_kernel, count, levels, chunks),
        in_specs=[pl.BlockSpec(memory_space=pltpu.HBM)] * 11,
        out_specs=(vmem, vmem, vmem),
        out_shape=(
            pltpu.VMEM((rows, cols), F32),
            pltpu.VMEM((count * per, 128), F32),
            pltpu.VMEM((1, part), jnp.int32),
        ),
        scratch_shapes=[
            V((rows, cols), F32),
            *[V((rows, width), F32)] * 9,
            V((2, rows, width), F32),
            V((5, width, width), BF16),
            V((2, levels, points, width), F32),
            V((2, levels, width), F32),
            *[V((padded, 2 * width), F32)] * 2,
            *[V((2, padded, width), F32)] * 2,
            V((2, ne), F32),
            V((1, ne), F32),
            V((4, ne), jnp.int32),
            V((4, ne), jnp.int32),
            V((1, cols), F32),
            V((1, points), F32),
            V((tracers, points), F32),
            V((1, points), F32),
            V((1, cols), jnp.int32),
            V((1, cols), jnp.int32),
            V((4, ne), jnp.int32),
            V((4, ne), jnp.int32),
            V((1, ne), F32),
            V((1, ne), F32),
            V((8, cols), jnp.int32),
            V((count, per, 128), F32),
            V((count, per, 128), F32),
            sems(4, len(chunks)),
            sems(4, len(chunks)),
            sems(4),
            sems(4),
            sems(3),
            sems(3),
            sems(count),
            sems(count),
            sems(fields),
            sems(10),
        ],
        compiler_params=pltpu.CompilerParams(
            collective_id=0, has_side_effects=True, vmem_limit_bytes=40 * 1024 * 1024
        ),
        name="step",
    )(
        *(
            pltpu.with_memory_space_constraint(a, pltpu.HBM)
            for a in (
        air_state,
        metric,
        jacobian[None, :],
        edge_nbr,
        edge_side,
        coszen[None, :],
        kappa_base[None, :],
        band_kappa.T,
        solar_weight[None, :],
        stretch_src[None, :],
        stretch_pos[None, :],
            )
        )
    )
    new, flux = pl.pallas_call(
        functools.partial(store_kernel, levels),
        in_specs=[vmem] * 3,
        out_specs=(anywhere, anywhere),
        out_shape=(
            jax.ShapeDtypeStruct(air_state.shape, F32),
            jax.ShapeDtypeStruct((1, part), F32),
        ),
        scratch_shapes=[V((1, part), F32), sems(fields + 1)],
        compiler_params=pltpu.CompilerParams(vmem_limit_bytes=8 * 1024 * 1024),
        name="store",
    )(new, table, index)
    return (new, flux.reshape(part))


def solution(mesh):
    return jax.shard_map(
        local,
        mesh=mesh,
        in_specs=(
            P(None, "lev", "sfc"),
            P(None, "sfc"),
            P("sfc"),
            P(None, "sfc"),
            P(None, "sfc"),
            P("sfc"),
            P(),
            P(),
            P(),
            P("sfc"),
            P("sfc"),
        ),
        out_specs=(P(None, "lev", "sfc"), P(("sfc", "lev"))),
        check_vma=False,
    )
```

```python
import functools

import jax
import jax.numpy as jnp
import numpy as np
from jax import lax
from jax.experimental import pallas as pl
from jax.experimental.pallas import tpu as pltpu
from jax.sharding import PartitionSpec as P

NODES = 16
GLL_POINTS = np.array([-1.0, -1.0 / np.sqrt(5.0), 1.0 / np.sqrt(5.0), 1.0])
EDGE_NODES = ((4, 8), (13, 14), (11, 7), (2, 1))
STEP_DYN = 0.2
DEPTH_UNIT = 0.05
HEAT_SCALE = 0.1
FLUX_SCALE = 0.02
F32 = jnp.float32
BF16 = jnp.bfloat16


def derivative_matrix():
    spacing = GLL_POINTS[:, None] - GLL_POINTS[None, :]
    unit_diag = np.eye(4)
    safe_space = np.where(unit_diag > 0, 1.0, spacing)
    weights_row = np.prod(safe_space, axis=1)
    derivative = weights_row[:, None] / weights_row[None, :] / safe_space
    inverse_gap = np.where(unit_diag > 0, 0.0, 1.0 / safe_space)
    return np.where(unit_diag > 0, inverse_gap.sum(axis=1)[:, None], derivative)


def split2(x):
    high = x.astype(BF16)
    return high, (x - high.astype(F32)).astype(BF16)


def dot(a, b):
    return jnp.dot(a, b, preferred_element_type=F32)


MESH = pl.DeviceIdType.MESH
EDGES = tuple(n for pair in EDGE_NODES for n in pair)
INNER = tuple(n for n in range(NODES) if n not in EDGES)


def column(row):
    n = row.shape[1]
    same = lax.broadcasted_iota(jnp.int32, (n, n), 0) == lax.broadcasted_iota(
        jnp.int32, (n, n), 1
    )
    return jnp.sum(jnp.where(same, jnp.broadcast_to(row, (n, n)), 0.0), axis=1, keepdims=True)


def log2(n):
    assert n & (n - 1) == 0
    return n.bit_length() - 1


def mix(a, b):
    return lax.dot_general(a, b, (((0,), (0,)), ((), ())), preferred_element_type=F32)


def spread_rates(bands, rows, per):
    high, low = split2(-DEPTH_UNIT * bands)
    shape = (bands.shape[0], 3 * rows)
    tracer = lax.broadcasted_iota(jnp.int32, shape, 0)
    lane = lax.broadcasted_iota(jnp.int32, shape, 1)
    third = jnp.where(lane >= rows, 1, 0) + jnp.where(lane >= 2 * rows, 1, 0)
    hit = (lane - third * rows) >> log2(per) == tracer
    one = lambda m: jnp.where(m, 1.0, 0.0).astype(BF16)
    return mix(high, one(hit & (third < 2))) + mix(low, one(hit & (third == 2)))


def stack3(x):
    high = x.astype(BF16).astype(F32)
    return jnp.concatenate([high, x - high, high], axis=0).astype(BF16)


def step_kernel(
    count,
    levels,
    chunks,
    state_ref,
    metric_hbm,
    jac_hbm,
    nbr_hbm,
    side_hbm,
    sun_hbm,
    base_hbm,
    band_hbm,
    weight_hbm,
    src_hbm,
    pos_hbm,
    new_ref,
    table_ref,
    index_ref,
    x_ref,
    seconds,
    firsts,
    direct_buf,
    relay_buf,
    cross_buf,
    mixed,
    mixed_buf,
    far0,
    far1,
    merged,
    choices,
    glow,
    heats,
    sq_inner,
    other_inner,
    sq_edge,
    other_edge,
    metric_ref,
    jac_ref,
    nbr_ref,
    side_ref,
    sun_ref,
    base_ref,
    band_ref,
    weight_ref,
    src_ref,
    pos_ref,
    their_nbr,
    their_side,
    direct_jac,
    relay_jac,
    spots,
    outbox,
    inbox,
    edge_send,
    edge_recv,
    meta_send,
    meta_recv,
    swap_send,
    swap_recv,
    flux_send,
    flux_recv,
    in_sem,
    small_sem,
):
    rows, cols = x_ref.shape
    ne = cols // NODES
    fields = rows // levels
    tracers = band_ref.shape[0]
    skip = rows - tracers * levels
    width = 4 * ne
    me, lev = lax.axis_index("sfc"), lax.axis_index("lev")
    odd = lax.rem(me, 2)
    partner = me + 1 - 2 * odd
    onward = lax.rem(me + count + 2 - 4 * odd, count)
    backward = lax.rem(me + count - 2 + 4 * odd, count)
    barrier = pltpu.get_barrier_semaphore()

    def greet(step, carry):
        pl.semaphore_signal(
            barrier, inc=1, device_id=(lax.rem(me + step, count), lev), device_id_type=MESH
        )
        return carry

    lax.fori_loop(1, count, greet, 0)
    pl.semaphore_signal(barrier, inc=1, device_id=(me, 1 - lev), device_id_type=MESH)

    small = [
        pltpu.make_async_copy(a, b, small_sem.at[i])
        for i, (a, b) in enumerate(
            (
                (metric_hbm, metric_ref),
                (jac_hbm, jac_ref),
                (nbr_hbm, nbr_ref),
                (side_hbm, side_ref),
                (band_hbm, band_ref),
                (base_hbm, base_ref),
                (weight_hbm, weight_ref),
                (sun_hbm, sun_ref),
                (pos_hbm, pos_ref),
                (src_hbm, src_ref),
            )
        )
    ]

    def fetch(f):
        return pltpu.make_async_copy(
            state_ref.at[f], x_ref.at[f * levels : (f + 1) * levels], in_sem.at[f]
        )

    for copy in small[:2]:
        copy.start()
    for start, stop in chunks:
        for f in range(start // levels, stop // levels):
            fetch(f).start()
        if start == chunks[0][0]:
            for copy in small[2:]:
                copy.start()

    d = derivative_matrix()

    def remote(src, dst, send, recv, to):
        return pltpu.make_async_remote_copy(
            src, dst, send, recv, device_id=to, device_id_type=MESH
        )

    def edge_copy(kind, src, dst, to):
        def make(c):
            part = slice(*chunks[c])
            return remote(
                src.at[part], dst.at[part], edge_send.at[kind, c], edge_recv.at[kind, c], (to, lev)
            )

        return make

    direct = edge_copy(0, seconds, direct_buf, partner)
    relay = edge_copy(1, direct_buf, relay_buf, onward)
    cross = edge_copy(2, firsts, cross_buf, backward)
    blend = edge_copy(3, mixed, mixed_buf, partner)
    meta = [
        remote(a, b, meta_send.at[i], meta_recv.at[i], (to, lev))
        for i, (a, b, to) in enumerate(
            (
                (jac_ref, direct_jac, partner),
                (direct_jac, relay_jac, onward),
                (nbr_hbm, their_nbr, partner),
                (side_hbm, their_side, partner),
            )
        )
    ]

    small[0].wait()
    small[1].wait()
    m0 = jnp.broadcast_to(STEP_DYN * metric_ref[0:1, :], (8, ne))
    m1 = jnp.broadcast_to(STEP_DYN * metric_ref[1:2, :], (8, ne))

    def advance(r, carry):
        sl = pl.ds(pl.multiple_of(r * 8, 8), 8)
        x = [x_ref[sl, n * ne : (n + 1) * ne] for n in range(NODES)]
        out = []
        for i in range(4):
            for j in range(4):
                one = sum(float(d[i, a]) * x[4 * a + j] for a in range(4))
                two = sum(float(d[j, a]) * x[4 * i + a] for a in range(4))
                out.append(x[4 * i + j] + (m0 * one + m1 * two))
        for n in INNER:
            new_ref[sl, n * ne : (n + 1) * ne] = out[n]
        for k, (a, b) in enumerate(EDGE_NODES):
            seconds[sl, k * ne : (k + 1) * ne] = out[b]
            firsts[sl, k * ne : (k + 1) * ne] = out[a]
        return carry

    last = len(chunks) - 1
    for c, (start, stop) in enumerate(chunks):
        for f in range(start // levels, stop // levels):
            fetch(f).wait()
        lax.fori_loop(start // 8, stop // 8, advance, 0)
        if c == 0:
            pl.semaphore_wait(barrier, count)
            for i in (0, 2, 3):
                meta[i].start()
        direct(c).start()
        if c < last:
            cross(c).start()

    def swap(part, a, b):
        return remote(a, b, swap_send.at[part], swap_recv.at[part], (me, 1 - lev))

    thick = tracers * levels
    padded = other_inner.shape[0]
    row = lax.broadcasted_iota(jnp.int32, (padded, 3 * thick), 0)
    lane = lax.broadcasted_iota(jnp.int32, (padded, 3 * thick), 1)
    lane = jnp.where(lane >= thick, lane - thick, lane)
    level_sum = jnp.where(lane >> log2(levels) == row, 1.0, 0.0).astype(BF16)

    def inner_tracers(part):
        nodes = INNER[part * 4 : part * 4 + 4]
        return jnp.concatenate(
            [new_ref[skip:, n * ne : (n + 1) * ne] for n in nodes], axis=1
        )

    for part in range(2):
        values = inner_tracers(part)
        sq_inner[:, part * width : (part + 1) * width] = dot(
            level_sum, stack3(values * values)
        )
    inner_swap = swap(0, sq_inner, other_inner)
    inner_swap.start()
    edge_swaps = [swap(1 + p, sq_edge.at[p], other_edge.at[p]) for p in range(2)]

    for copy in small[2:]:
        copy.wait()
    top = jnp.where(lev == 0, 1.0, 0.0).astype(F32)
    rates = spread_rates(band_ref[...], thick, levels)
    own_level = lax.rem(lax.broadcasted_iota(jnp.int32, rates.shape, 1), levels)
    own_rates = [jnp.where(own_level <= l, rates, 0.0).astype(BF16) for l in range(levels)]
    sum_rates = spread_rates(band_ref[...], padded, 1).astype(BF16)
    base = -DEPTH_UNIT * column(base_ref[...])
    weight = column(weight_ref[...])

    total_nodes = count * ne

    def spot_of(nbr, side, where):
        near = nbr - (where - 1) * ne
        near = jnp.where(near < 0, near + total_nodes, near)
        near = jnp.where(near >= total_nodes, near - total_nodes, near)
        window = jnp.where(near >= ne, 1, 0) + jnp.where(near >= 2 * ne, 1, 0)
        spot = window * (width - ne) + side * ne + near
        return jnp.concatenate([spot[k : k + 1, :] for k in range(4)], axis=1)

    def choose(i, target, w):
        lanes = lax.broadcasted_iota(jnp.int32, (width, width), 0) + w * width
        choices[i] = jnp.where(lanes == target, 1.0, 0.0).astype(BF16)

    def pick(values, i):
        n = values.shape[0]
        high, low = split2(values)
        both = dot(jnp.concatenate([high, low], axis=0), choices[i])
        return both[:n] + both[n:]

    def pick_jac(ref, i):
        wide = jnp.concatenate([jnp.broadcast_to(ref[...], (16, ne))] * 4, axis=1)
        return pick(wide, i)[0:1]

    def own_glow(slot, stacked):
        for l in range(levels):
            depth = dot(own_rates[l], stacked) + (l + 1.0) * base
            glow[slot, l] = weight * jnp.exp(depth)

    def finish(slot, other, sun):
        far = jnp.exp(dot(sum_rates, stack3(other)) + levels * base)
        keep = top + (1.0 - top) * far
        total = lambda v: jnp.sum(v, axis=0, keepdims=True)
        above = total(weight * keep)
        heat = []
        for l in range(levels):
            below = total(glow[slot, l] * keep)
            heat.append(HEAT_SCALE * sun * (above - below))
            above = below
        ground = FLUX_SCALE * sun * total(glow[slot, levels - 1] * far)
        return jnp.concatenate(heat, axis=0), ground

    def join(ref, row, nodes):
        return jnp.concatenate(
            [ref[row : row + 1, n * ne : (n + 1) * ne] for n in nodes], axis=1
        )

    lines = table_ref.shape[0]
    per = lines // count
    shift = log2(cols)

    def runs(device, place):
        ids = lax.broadcasted_iota(jnp.int32, (count, cols), 0)
        match = ids == device
        place = place.astype(F32)
        least = jnp.min(jnp.where(match, place, 1e9), axis=1, keepdims=True)
        return (place - jnp.sum(jnp.where(match, least, 0.0), axis=0, keepdims=True)).astype(
            jnp.int32
        )

    goes = pos_ref[...] >> shift
    rank = runs(goes, pos_ref[...])
    spots[0:1, :] = goes * per + (rank >> 7)
    spots[1:2, :] = rank & 127
    comes = src_ref[...] >> shift
    rank = runs(comes, lax.broadcasted_iota(jnp.int32, (1, cols), 1))
    spots[2:3, :] = comes * (per * 128) + rank
    taken = index_ref.shape[1]
    index_ref[...] = spots[2:3, pl.ds(pl.multiple_of(lev * taken, 128), taken)]

    def scatter(ground, nodes):
        line, lane = join(spots, 0, nodes), join(spots, 1, nodes)
        n = line.shape[1]
        there = lax.broadcasted_iota(jnp.int32, (lines, n), 0) == line
        high, _ = split2(ground)
        low, tail = split2(ground - high.astype(F32))
        parts = [jnp.where(there, v.astype(F32), 0.0) for v in (high, low, tail)]
        onehot = jnp.where(
            lax.broadcasted_iota(jnp.int32, (128, n), 0) == lane, 1.0, 0.0
        ).astype(BF16)
        out = lax.dot_general(
            jnp.concatenate(parts, axis=0).astype(BF16),
            onehot,
            (((1,), (1,)), ((), ())),
            preferred_element_type=F32,
        )
        return out[:lines] + out[lines : 2 * lines] + out[2 * lines :]

    def inner_part(part):
        nodes = INNER[part * 4 : part * 4 + 4]
        values = inner_tracers(part)
        own_glow(part, stack3(values * values))
        other = other_inner[:, part * width : (part + 1) * width]
        heat, ground = finish(part, other, jnp.maximum(join(sun_ref, 0, nodes), 0.0))
        for s, n in enumerate(nodes):
            lanes = slice(n * ne, (n + 1) * ne)
            new_ref[2 * levels : 3 * levels, lanes] = (
                new_ref[2 * levels : 3 * levels, lanes] + heat[:, s * ne : (s + 1) * ne]
            )
        return scatter(ground, nodes)

    target = spot_of(nbr_ref[...], side_ref[...], me)
    choose(0, target, 1)
    far1[...] = pick(firsts[...], 0)
    far0[...] = pick(seconds[...], 0)
    own_jac = pick_jac(jac_ref, 0)
    inner_swap.wait_recv()
    table = inner_part(0)

    def forward(c):
        direct(c).wait_recv()
        relay(c).start()

    meta[0].wait_recv()
    meta[1].start()
    forward(0)
    forward(1)
    cross(last).start()
    meta[2].wait_recv()
    meta[3].wait_recv()
    theirs = spot_of(their_nbr[...], their_side[...], partner)
    choose(1, theirs, 2 * odd)
    choose(2, theirs, 2 - 2 * odd)
    mixed[...] = pick(firsts[...], 1)

    def answer(c):
        part = slice(*chunks[c])
        cross(c).wait_recv()
        mixed[part] = mixed[part] + pick(cross_buf[part], 2)
        blend(c).start()

    for c in range(last):
        answer(c)
        if 2 + c < last:
            forward(2 + c)
    forward(last)
    answer(last)
    table = table + inner_part(1)

    choose(3, target, 2 - 2 * odd)
    choose(4, target, 2 * odd)
    for c in range(last):
        part = slice(*chunks[c])
        far0[part] = far0[part] + pick(direct_buf[part], 3)
    meta[1].wait_recv()
    far_jac = own_jac + pick_jac(direct_jac, 3) + pick_jac(relay_jac, 4)
    mine = jnp.concatenate([jac_ref[...]] * 4, axis=1)
    own_part, far_part = mine / (mine + far_jac), far_jac / (mine + far_jac)
    nodes_of = [[a for a, _ in EDGE_NODES], [b for _, b in EDGE_NODES]]

    def put(p, part, values):
        for k, n in enumerate(nodes_of[p]):
            new_ref[part, n * ne : (n + 1) * ne] = values[:, k * ne : (k + 1) * ne]

    def merge(p, c):
        part = slice(*chunks[c])
        if p == 0:
            relay(c).wait_recv()
            far, own = far0[part] + pick(relay_buf[part], 4), firsts[part]
        else:
            blend(c).wait_recv()
            far, own = far1[part] + mixed_buf[part], seconds[part]
        return own_part * own + far_part * far

    def settle(p, c):
        part = slice(*chunks[c])
        values = merge(p, c)
        merged[p, part] = values
        put(p, part, values)

    def share(p):
        values = merged[p, skip:]
        stacked = stack3(values * values)
        sq_edge[p] = dot(level_sum, stacked)
        edge_swaps[p].start()
        own_glow(p, stacked)

    def shine(p):
        edge_swaps[p].wait_recv()
        sun = jnp.maximum(join(sun_ref, 0, nodes_of[p]), 0.0)
        heats[p], ground = finish(p, other_edge[p], sun)
        return scatter(ground, nodes_of[p])

    for c in range(last):
        settle(0, c)
    share(0)
    for c in range(last):
        settle(1, c)
    share(1)
    table = table + shine(0)
    table = table + shine(1)
    for k in range(count):
        outbox[k] = table[k * per : (k + 1) * per]

    def send(step):
        to = lax.rem(me + step, count)
        return remote(
            outbox.at[to], inbox.at[me], flux_send.at[step], flux_recv.at[me], (to, lev)
        )

    def arrive(step):
        peer = lax.rem(me + step, count)
        return remote(
            outbox.at[peer], inbox.at[peer], flux_send.at[step], flux_recv.at[peer], (peer, lev)
        )

    def start_send(step, carry):
        send(step).start()
        return carry

    def finish_send(step, carry):
        send(step).wait_send()
        arrive(step).wait_recv()
        return carry

    lax.fori_loop(1, count, start_send, 0)
    inbox[me] = outbox[me]

    part = slice(*chunks[last])
    far0[part] = far0[part] + pick(direct_buf[part], 3)
    for p in range(2):
        values = merge(p, last)
        warm = slice(2 * levels, 3 * levels)
        values = jnp.concatenate(
            [values[: 2 * levels], values[warm] + heats[p], values[3 * levels :]], axis=0
        )
        put(p, part, values)
    for copy in meta + [inner_swap] + edge_swaps:
        copy.wait_send()
    for c in range(last + 1):
        for kind in (direct, relay, cross, blend):
            kind(c).wait_send()
    lax.fori_loop(1, count, finish_send, 0)
    for k in range(count):
        table_ref[k * per : (k + 1) * per, :] = inbox[k]


def store_kernel(levels, state_ref, table_ref, index_ref, new_ref, flux_out, flux_ref, sem):
    fields = state_ref.shape[0] // levels

    def store(f):
        return pltpu.make_async_copy(
            state_ref.at[f * levels : (f + 1) * levels], new_ref.at[f], sem.at[f]
        )

    for f in range(fields):
        store(f).start()
    taken = flux_ref.shape[1]
    lines = table_ref.shape[0]
    index = index_ref[...]
    here = lax.broadcasted_iota(jnp.int32, (lines, taken), 0) == index >> 7
    onehot = jnp.where(here, 1.0, 0.0).astype(BF16)
    mask = lax.broadcasted_iota(jnp.int32, (128, taken), 0) == (index & 127)
    values = table_ref[...].T
    high, _ = split2(values)
    low, tail = split2(values - high.astype(F32))
    picked = dot(high, onehot) + dot(low, onehot) + dot(tail, onehot)
    flux_ref[...] = jnp.sum(jnp.where(mask, picked, 0.0), axis=0, keepdims=True)
    give = pltpu.make_async_copy(flux_ref, flux_out, sem.at[fields])
    give.start()
    for f in range(fields):
        store(f).wait()
    give.wait()


def row_chunks(rows, skip):
    groups = (rows - skip) // 8
    edges = [skip + 8 * round(groups * share) for share in (0.0, 0.2, 0.5, 0.8, 1.0)]
    return tuple(zip(edges[:-1], edges[1:])) + ((0, skip),)


def local(
    air_state,
    metric,
    jacobian,
    edge_nbr,
    edge_side,
    coszen,
    kappa_base,
    band_kappa,
    solar_weight,
    stretch_pos,
    stretch_src,
):
    fields, levels, cols = air_state.shape
    ne = cols // NODES
    rows = fields * levels
    width = 4 * ne
    points, tracers = band_kappa.shape
    padded = -(-tracers // 8) * 8
    count = lax.axis_size("sfc")
    part = cols // lax.axis_size("lev")
    chunks = row_chunks(rows, rows - tracers * levels)
    per = max(2 * cols // count // 128, 1)
    anywhere = pl.BlockSpec(memory_space=pl.ANY)
    vmem = pl.BlockSpec(memory_space=pltpu.VMEM)
    V = pltpu.VMEM
    sems = lambda *shape: pltpu.SemaphoreType.DMA(shape)
    new, table, index = pl.pallas_call(
        functools.partial(step_kernel, count, levels, chunks),
        in_specs=[pl.BlockSpec(memory_space=pltpu.HBM)] * 11,
        out_specs=(vmem, vmem, vmem),
        out_shape=(
            pltpu.VMEM((rows, cols), F32),
            pltpu.VMEM((count * per, 128), F32),
            pltpu.VMEM((1, part), jnp.int32),
        ),
        scratch_shapes=[
            V((rows, cols), F32),
            *[V((rows, width), F32)] * 9,
            V((2, rows, width), F32),
            V((5, width, width), BF16),
            V((2, levels, points, width), F32),
            V((2, levels, width), F32),
            *[V((padded, 2 * width), F32)] * 2,
            *[V((2, padded, width), F32)] * 2,
            V((2, ne), F32),
            V((1, ne), F32),
            V((4, ne), jnp.int32),
            V((4, ne), jnp.int32),
            V((1, cols), F32),
            V((1, points), F32),
            V((tracers, points), F32),
            V((1, points), F32),
            V((1, cols), jnp.int32),
            V((1, cols), jnp.int32),
            V((4, ne), jnp.int32),
            V((4, ne), jnp.int32),
            V((1, ne), F32),
            V((1, ne), F32),
            V((8, cols), jnp.int32),
            V((count, per, 128), F32),
            V((count, per, 128), F32),
            sems(4, len(chunks)),
            sems(4, len(chunks)),
            sems(4),
            sems(4),
            sems(3),
            sems(3),
            sems(count),
            sems(count),
            sems(fields),
            sems(10),
        ],
        compiler_params=pltpu.CompilerParams(
            collective_id=0, has_side_effects=True, vmem_limit_bytes=40 * 1024 * 1024
        ),
        name="step",
    )(
        *(
            pltpu.with_memory_space_constraint(a, pltpu.HBM)
            for a in (
        air_state,
        metric,
        jacobian[None, :],
        edge_nbr,
        edge_side,
        coszen[None, :],
        kappa_base[None, :],
        band_kappa.T,
        solar_weight[None, :],
        stretch_src[None, :],
        stretch_pos[None, :],
            )
        )
    )
    new, flux = pl.pallas_call(
        functools.partial(store_kernel, levels),
        in_specs=[vmem] * 3,
        out_specs=(anywhere, anywhere),
        out_shape=(
            jax.ShapeDtypeStruct(air_state.shape, F32),
            jax.ShapeDtypeStruct((1, part), F32),
        ),
        scratch_shapes=[V((1, part), F32), sems(fields + 1)],
        compiler_params=pltpu.CompilerParams(vmem_limit_bytes=8 * 1024 * 1024),
        name="store",
    )(new, table, index)
    return (new, flux.reshape(part))


def solution(mesh):
    return jax.shard_map(
        local,
        mesh=mesh,
        in_specs=(
            P(None, "lev", "sfc"),
            P(None, "sfc"),
            P("sfc"),
            P(None, "sfc"),
            P(None, "sfc"),
            P("sfc"),
            P(),
            P(),
            P(),
            P("sfc"),
            P("sfc"),
        ),
        out_specs=(P(None, "lev", "sfc"), P(("sfc", "lev"))),
        check_vma=False,
    )
```
